512 devices in a mesh: ctx: 64 (over z, x, core), tp: 8 (over y).
Axes of the slice: x: 4, y: 8, z: 8, core: 2. Of those that a mesh axis runs over, the one named last changes fastest.
Arguments:
- ctx_queries: bfloat16 [16384, 4096], P('ctx', 'tp'), may hold values from -5 to 5
- ctx_keys: bfloat16 [16384, 1024], P('ctx', 'tp'), may hold values from -5 to 5
- ctx_values: bfloat16 [16384, 1024], P('ctx', 'tp'), may hold values from -18 to 18
- query_queries: bfloat16 [512, 4096], P(None, 'tp'), may hold values from -5 to 5
- query_keys: bfloat16 [512, 1024], P('ctx', 'tp'), may hold values from -5 to 5
- query_values: bfloat16 [512, 1024], P('ctx', 'tp'), may hold values from -18 to 18
- out_weight: bfloat16 [4096, 4096], P('tp', 'ctx'), may hold values from -0.09375 to 0.09375
Outputs:
- ctx_out: bfloat16 [16384, 4096], P('ctx', 'tp')
- query_out: bfloat16 [512, 4096], P('tp', 'ctx')
The draws below stay inside these ranges and needn't reach their ends.
All inputs are finite; a program needn't handle non-finite values.
Results may differ from the reference program's by a relative error of at most 0.0049.
Values may be sent and summed in bfloat16 or wider, within the bound.
No kernel may reach another device: no remote copies, remote signals or barrier semaphores. Data moves between devices by JAX's collectives and lax.ppermute only.
A program may use at most 192 MiB of HBM per device.

```python
import jax
import jax.numpy as jnp
from jax import lax

D = 4096
HEADS = 32
KV_HEADS = 8
HD = 128
BLK = 256
QL = 512
CONTEXT = 16384
N_CTX = 64


def base_field(key, rows, cols):
    return jnp.clip(1.565 * jax.random.normal(key, (rows, cols), jnp.float32), -5.0, 5.0)


def draw_ctx_keys(key, part):
    field = base_field(jax.random.fold_in(key, 11), CONTEXT, KV_HEADS * HD)
    return field.astype(jnp.bfloat16)


def draw_ctx_queries(key, part):
    field = base_field(jax.random.fold_in(key, 23), CONTEXT, HEADS * HD)
    return field.astype(jnp.bfloat16)


def draw_query_queries(key, part):
    field = base_field(jax.random.fold_in(key, 37), QL, HEADS * HD)
    return field.astype(jnp.bfloat16)


def block_levels(own_key, extent, cuts, low, top_value):
    gain, own = 1.0, jax.random.fold_in(own_key, 6)
    for dim, blocks in cuts:
        steps = jnp.exp(jax.random.uniform(jax.random.fold_in(own, dim), (blocks,), jnp.float32, low / len(cuts), top_value / len(cuts)))
        gain = gain * jnp.repeat(steps, extent[dim] // blocks).reshape([-1 if axis == dim else 1 for axis in range(len(extent))])
    return gain


def gaussian(key, dims, width, limit, split=(), kind=jnp.bfloat16):
    factor_of = block_levels(key, dims, split, -0.22, 0.18) if split else 1.0
    drawn = jax.random.normal(key, dims, jnp.float32) * width * factor_of
    return jnp.minimum(jnp.maximum(drawn, -limit), limit).astype(kind)


def setup_inputs(seed: int = 0) -> dict:
    splits = jax.random.split(jax.random.key(seed), 8)
    return {
        "ctx_queries": draw_ctx_queries(jax.random.fold_in(splits[7], 71), 0),
        "ctx_keys": draw_ctx_keys(jax.random.fold_in(splits[7], 71), 0),
        "ctx_values": gaussian(splits[2], (CONTEXT, KV_HEADS * HD), 3.0, 18.0, ((0, 64), (1, 8))),
        "query_queries": draw_query_queries(jax.random.fold_in(splits[7], 71), 0),
        "query_keys": gaussian(splits[4], (QL, KV_HEADS * HD), 1.565, 5.0, ((0, 64), (1, 8))),
        "query_values": gaussian(splits[5], (QL, KV_HEADS * HD), 3.0, 18.0, ((0, 64), (1, 8))),
        "out_weight": gaussian(splits[6], (HEADS * HD, D), (HEADS * HD) ** -0.5, 0.09375, ((0, 8), (1, 64))),
    }


def attend_part(query_part, key_part, value_part, visible):
    scale = HD ** -0.5
    scores = jnp.einsum('tkgd,skd->tkgs', query_part.astype(jnp.float32), key_part.astype(jnp.float32)) * scale
    scores = jnp.where(visible[:, None, None, :], scores, -jnp.inf)
    top = jnp.max(scores, axis=-1)
    weights = jnp.exp(scores - top[..., None])
    total = jnp.sum(weights, axis=-1)
    probs = weights.astype(jnp.bfloat16)
    summed = jnp.einsum('tkgs,skd->tkgd', probs.astype(jnp.float32), value_part.astype(jnp.float32))
    return top, total, summed


def combine_parts(first, second):
    top = jnp.maximum(first[0], second[0])
    left = jnp.exp(first[0] - top)
    right = jnp.exp(second[0] - top)
    total = first[1] * left + second[1] * right
    summed = first[2] * left[..., None] + second[2] * right[..., None]
    return top, total, summed


def reference(ctx_queries, ctx_keys, ctx_values, query_queries, query_keys, query_values, out_weight):
    group = HEADS // KV_HEADS
    share = QL // N_CTX
    ctx_grid = ctx_queries.reshape(N_CTX, BLK, KV_HEADS, group, HD)
    key_grid = ctx_keys.reshape(N_CTX, BLK, KV_HEADS, HD)
    value_grid = ctx_values.reshape(N_CTX, BLK, KV_HEADS, HD)
    query_grid = query_queries.reshape(QL, KV_HEADS, group, HD)
    qkey_grid = query_keys.reshape(N_CTX, share, KV_HEADS, HD)
    qvalue_grid = query_values.reshape(N_CTX, share, KV_HEADS, HD)
    position = jnp.arange(BLK)
    causal = position[:, None] >= position[None, :]

    def context_block(block):
        key_rows = jnp.concatenate([key_grid[0], key_grid[block]], 0)
        value_rows = jnp.concatenate([value_grid[0], value_grid[block]], 0)
        anchor_seen = jnp.broadcast_to(block > 0, (BLK, BLK))
        visible = jnp.concatenate([anchor_seen, causal], 1)
        top, total, summed = attend_part(ctx_grid[block], key_rows, value_rows, visible)
        return (summed / total[..., None]).astype(jnp.bfloat16).reshape(BLK, HEADS * HD)

    ctx_out = lax.map(context_block, jnp.arange(N_CTX)).reshape(N_CTX * BLK, HEADS * HD)

    query_pos = jnp.arange(QL)

    def fold_block(carry, block):
        key_rows = jnp.concatenate([key_grid[block], qkey_grid[block]], 0)
        value_rows = jnp.concatenate([value_grid[block], qvalue_grid[block]], 0)
        key_pos = block * share + jnp.arange(share)
        visible = jnp.concatenate([jnp.ones((QL, BLK), dtype=bool), query_pos[:, None] >= key_pos[None, :]], 1)
        part = attend_part(query_grid, key_rows, value_rows, visible)
        return combine_parts(carry, part), None

    start = (jnp.full((QL, KV_HEADS, group), -jnp.inf, jnp.float32),
             jnp.zeros((QL, KV_HEADS, group), jnp.float32),
             jnp.zeros((QL, KV_HEADS, group, HD), jnp.float32))
    final, unused = lax.scan(fold_block, start, jnp.arange(N_CTX))
    attended = (final[2] / final[1][..., None]).astype(jnp.bfloat16).reshape(QL, HEADS * HD)
    query_out = jnp.dot(attended, out_weight, preferred_element_type=jnp.float32).astype(jnp.bfloat16)
    return ctx_out, query_out
```

```python
import jax
import jax.numpy as jnp
from jax import lax
from jax.experimental import pallas as pl
from jax.experimental.pallas import tpu as pltpu
from jax.sharding import Mesh
from jax.sharding import PartitionSpec as P

HD = 128
GROUP = 4
BLK = 256
QL = 512
SHARE = 8
PEERS = 32
HALF = QL // 2
SCALE = HD**-0.5
F32 = jnp.float32
BF16 = jnp.bfloat16

STATS = GROUP * HD
ANCHOR = STATS + HD
FIRST = ANCHOR + 2 * HD
SECOND = GROUP * HD + 2 * HD


def nt(a, b):
    return lax.dot_general(a, b, (((1,), (1,)), ((), ())), preferred_element_type=F32)


def nn(a, b):
    return lax.dot_general(a, b, (((1,), (0,)), ((), ())), preferred_element_type=F32)


def query_kernel(where, rows_ref, own_ref, mate_ref, out_ref):
    core, block, mate = where[0], where[1], where[2]
    rows = rows_ref[...].reshape(HALF, GROUP * HD)
    own_keys, own_values = own_ref[0:BLK, :], own_ref[BLK : 2 * BLK, :]
    mate_keys, mate_values = mate_ref[0:BLK, :], mate_ref[BLK : 2 * BLK, :]
    own_tail = own_ref[2 * BLK : 2 * BLK + 2 * SHARE, :].astype(F32)
    mate_tail = mate_ref[2 * BLK : 2 * BLK + 2 * SHARE, :].astype(F32)
    tail_keys = jnp.concatenate([own_tail[:SHARE], mate_tail[:SHARE]], 0).astype(BF16)
    tail_values = jnp.concatenate([own_tail[SHARE:], mate_tail[SHARE:]], 0).astype(BF16)

    index = lax.broadcasted_iota(jnp.int32, (HALF, 2 * SHARE), 0)
    position = (index // 32) * 64 + core * 32 + index % 32
    column = lax.broadcasted_iota(jnp.int32, (HALF, 2 * SHARE), 1)
    key_position = jnp.where(column < SHARE, block * SHARE + column, mate * SHARE + column - SHARE)
    visible = position >= key_position

    lane = lax.broadcasted_iota(jnp.int32, (HALF, HD), 1)
    stats = jnp.zeros((HALF, HD), F32)
    for h in range(GROUP):
        q = rows[:, h * HD : (h + 1) * HD]
        own = nt(q, own_keys) * SCALE
        other = nt(q, mate_keys) * SCALE
        tail = jnp.where(visible, nt(q, tail_keys) * SCALE, -jnp.inf)
        top = jnp.maximum(
            jnp.max(jnp.maximum(own, other), axis=-1, keepdims=True),
            jnp.max(tail, axis=-1, keepdims=True),
        )
        top = jnp.ceil(top * 0.5) * 2.0
        own, other, tail = jnp.exp(own - top), jnp.exp(other - top), jnp.exp(tail - top)
        total = jnp.sum(own + other, axis=-1, keepdims=True) + jnp.sum(tail, axis=-1, keepdims=True)
        summed = (
            nn(own.astype(BF16), own_values)
            + nn(other.astype(BF16), mate_values)
            + nn(tail.astype(BF16), tail_values)
        )
        out_ref[:, h * HD : (h + 1) * HD] = summed.astype(BF16)
        high = total.astype(BF16).astype(F32)
        stats = jnp.where(lane == h, top, stats)
        stats = jnp.where(lane == GROUP + h, high, stats)
        stats = jnp.where(lane == 2 * GROUP + h, total - high, stats)
    out_ref[:, STATS:ANCHOR] = stats.astype(BF16)

    @pl.when(core == 0)
    def _():
        out_ref[:, ANCHOR : ANCHOR + HD] = own_keys
        out_ref[:, ANCHOR + HD : FIRST] = own_values

    @pl.when(core != 0)
    def _():
        out_ref[:, ANCHOR : ANCHOR + HD] = mate_keys
        out_ref[:, ANCHOR + HD : FIRST] = mate_values


def query_parts(where, query_queries, own, mate):
    taken = 2 * BLK + 2 * SHARE
    return pl.pallas_call(
        query_kernel,
        out_shape=jax.ShapeDtypeStruct((HALF, FIRST), BF16),
        grid_spec=pltpu.PrefetchScalarGridSpec(
            num_scalar_prefetch=1,
            grid=(1,),
            in_specs=[
                pl.BlockSpec((8, 1, 32, GROUP * HD), lambda i, where: (0, where[0], 0, 0)),
                pl.BlockSpec((taken, HD), lambda i, where: (0, 0)),
                pl.BlockSpec((taken, HD), lambda i, where: (0, 0)),
            ],
            out_specs=pl.BlockSpec((HALF, FIRST), lambda i, where: (0, 0)),
        ),
        cost_estimate=pl.CostEstimate(
            flops=4 * HALF * GROUP * 2 * BLK * HD,
            transcendentals=HALF * GROUP * 2 * BLK,
            bytes_accessed=1 << 20,
        ),
        name="query_parts",
    )(where, query_queries.reshape(8, 2, 32, GROUP * HD), own, mate)


def merge_kernel(parts_ref, out_ref):
    stats = parts_ref[:, :, STATS:ANCHOR].astype(F32)
    factor = jnp.exp(stats - jnp.max(stats, axis=0, keepdims=True))
    for h in range(GROUP):
        weight = jnp.broadcast_to(factor[:, :, h : h + 1], (PEERS, SHARE, HD))
        totals = jnp.sum(weight * stats, axis=0)
        total = totals[:, GROUP + h : GROUP + h + 1] + totals[:, 2 * GROUP + h : 2 * GROUP + h + 1]
        part = parts_ref[:, :, h * HD : (h + 1) * HD].astype(F32)
        attended = (jnp.sum(weight * part, axis=0) / total).astype(BF16)
        out_ref[:, :, h * HD : (h + 1) * HD] = jnp.broadcast_to(attended[None], (PEERS, SHARE, HD))
    anchor = parts_ref[0, :, ANCHOR:FIRST]
    out_ref[:, :, GROUP * HD :] = jnp.broadcast_to(anchor[None], (PEERS, SHARE, 2 * HD))


def merge_parts(parts):
    return pl.pallas_call(
        merge_kernel,
        out_shape=jax.ShapeDtypeStruct((PEERS, SHARE, SECOND), BF16),
        name="merge_parts",
    )(parts)


def project_kernel(where, rows_ref, own_ref, mate_ref, out_ref):
    core = where[0]
    rows = rows_ref[:, :, : GROUP * HD].astype(F32).reshape(8, 2, 16, GROUP * HD)
    upper = rows[:, 0].reshape(128, GROUP * HD).astype(BF16)
    lower = rows[:, 1].reshape(128, GROUP * HD).astype(BF16)
    own, mate = own_ref[...], mate_ref[...]
    zero = jnp.zeros_like(own)

    def packed(weight):
        left = jnp.concatenate([weight, zero], 1)
        right = jnp.concatenate([zero, weight], 1)
        return (nn(upper, left) + nn(lower, right)).reshape(8, 16, 128)

    out_ref[pl.ds(core, 1)] = packed(own)[None]
    out_ref[pl.ds(1 - core, 1)] = packed(mate)[None]


def project(where, rows, own, mate):
    return pl.pallas_call(
        project_kernel,
        out_shape=jax.ShapeDtypeStruct((2, 8, 16, 128), F32),
        in_specs=[
            pl.BlockSpec(memory_space=pltpu.SMEM),
            pl.BlockSpec(memory_space=pltpu.VMEM),
            pl.BlockSpec(memory_space=pltpu.VMEM),
            pl.BlockSpec(memory_space=pltpu.VMEM),
        ],
        name="project",
    )(where, rows, own, mate)


def context_kernel(where, q_ref, keys_ref, values_ref, anchor_ref, out_ref):
    has_anchor = where[1] > 0
    anchor = anchor_ref[:, :, GROUP * HD :].astype(F32).reshape(BLK, 2 * HD).astype(BF16)
    anchor_keys, anchor_values = anchor[:, :HD], anchor[:, HD:]
    keys, values = keys_ref[...], values_ref[...]
    row = lax.broadcasted_iota(jnp.int32, (BLK, BLK), 0)
    column = lax.broadcasted_iota(jnp.int32, (BLK, BLK), 1)
    for h in range(GROUP):
        q = q_ref[:, h * HD : (h + 1) * HD]
        own = jnp.where(row >= column, nt(q, keys) * SCALE, -jnp.inf)
        first = jnp.where(has_anchor, nt(q, anchor_keys) * SCALE, -jnp.inf)
        top = jnp.max(jnp.maximum(own, first), axis=-1, keepdims=True)
        own, first = jnp.exp(own - top), jnp.exp(first - top)
        total = jnp.sum(own + first, axis=-1, keepdims=True)
        summed = nn(own.astype(BF16), values) + nn(first.astype(BF16), anchor_values)
        out_ref[:, h * HD : (h + 1) * HD] = (summed / total).astype(BF16)


def context(where, queries, keys, values, gathered):
    return pl.pallas_call(
        context_kernel,
        out_shape=jax.ShapeDtypeStruct((BLK, GROUP * HD), BF16),
        in_specs=[pl.BlockSpec(memory_space=pltpu.SMEM)]
        + [pl.BlockSpec(memory_space=pltpu.VMEM)] * 4,
        cost_estimate=pl.CostEstimate(
            flops=4 * BLK * GROUP * 2 * BLK * HD,
            transcendentals=BLK * GROUP * 2 * BLK,
            bytes_accessed=1 << 20,
        ),
        name="context",
    )(where, queries, keys, values, gathered)


def finish_kernel(parts_ref, out_ref):
    for k in range(2):
        summed = jnp.sum(parts_ref[k * 8 : (k + 1) * 8], axis=0)
        out_ref[k * 32 : k * 32 + 16, :] = summed[:, :64].astype(BF16)
        out_ref[k * 32 + 16 : k * 32 + 32, :] = summed[:, 64:].astype(BF16)


def finish(parts):
    return pl.pallas_call(
        finish_kernel, out_shape=jax.ShapeDtypeStruct((64, 64), BF16), name="finish"
    )(parts)


def body(ctx_queries, ctx_keys, ctx_values, query_queries, query_keys, query_values, out_weight):
    core = lax.axis_index("core")
    block = (lax.axis_index("z") * 4 + lax.axis_index("x")) * 2 + core
    mate_block = block + 1 - 2 * core
    where = jnp.stack([core, block, mate_block]).astype(jnp.int32)

    wide = jnp.pad(out_weight, ((0, 0), (0, 64)))
    own = jnp.concatenate([ctx_keys, ctx_values, query_keys, query_values, wide], 0)
    mate = lax.ppermute(own, "core", [(0, 1), (1, 0)])
    mate_weight = mate[2 * BLK + 2 * SHARE :, :64]

    parts = query_parts(where, query_queries, own, mate)
    parts = lax.all_to_all(parts.reshape(PEERS, SHARE, FIRST), ("z", "x"), 0, 0)
    message = merge_parts(parts)
    gathered = lax.all_to_all(message, ("z", "x"), 0, 0)

    sums = project(where, gathered, out_weight, mate_weight)
    sums = lax.all_to_all(sums.reshape(16, 16, 128), ("core", "tp"), 0, 0)
    ctx_out = context(where, ctx_queries, ctx_keys, ctx_values, gathered)
    query_out = finish(sums)
    return (ctx_out, query_out)


def solution(mesh):
    fine = Mesh(mesh.devices.reshape(8, 4, 2, 8), ("z", "x", "core", "tp"))
    ctx = ("z", "x", "core")
    return jax.shard_map(
        body,
        mesh=fine,
        in_specs=(
            P(ctx, "tp"),
            P(ctx, "tp"),
            P(ctx, "tp"),
            P(None, "tp"),
            P(ctx, "tp"),
            P(ctx, "tp"),
            P("tp", ctx),
        ),
        out_specs=(P(ctx, "tp"), P("tp", ctx)),
        check_vma=False,
    )
```

```python
import jax
import jax.numpy as jnp
from jax import lax
from jax.experimental import pallas as pl
from jax.experimental.pallas import tpu as pltpu
from jax.sharding import Mesh
from jax.sharding import PartitionSpec as P

HD = 128
GROUP = 4
BLK = 256
QL = 512
SHARE = 8
PEERS = 32
HALF = QL // 2
SCALE = HD**-0.5
F32 = jnp.float32
BF16 = jnp.bfloat16

STATS = GROUP * HD
ANCHOR = STATS + HD
FIRST = ANCHOR + 2 * HD
SECOND = GROUP * HD + 2 * HD


TAIL = 2 * BLK
WEIGHT = TAIL + 2 * SHARE
PACKED = WEIGHT + GROUP * 64


def nt(a, b):
    return lax.dot_general(a, b, (((1,), (1,)), ((), ())), preferred_element_type=F32)


def nn(a, b):
    return lax.dot_general(a, b, (((1,), (0,)), ((), ())), preferred_element_type=F32)


def vmem(array):
    return pltpu.with_memory_space_constraint(array, pltpu.VMEM)


IN_VMEM = pl.BlockSpec(memory_space=pltpu.VMEM)


def position_of():
    core = lax.axis_index("core")
    return core, (lax.axis_index("z") * 4 + lax.axis_index("x")) * 2 + core


def pack_kernel(
    keys_ref, values_ref, query_keys_ref, query_values_ref, weight_ref, rows_ref, out_ref, half_ref
):
    out_ref[0:BLK, :] = keys_ref[...]
    out_ref[BLK : 2 * BLK, :] = values_ref[...]
    tail = jnp.concatenate([query_keys_ref[...].astype(F32), query_values_ref[...].astype(F32)], 0)
    out_ref[TAIL:WEIGHT, :] = tail.astype(BF16)
    for h in range(GROUP):
        start = WEIGHT + h * 64
        out_ref[start : start + 64, :] = weight_ref[:, h * HD : (h + 1) * HD]
    core, unused = position_of()
    half_ref[...] = rows_ref[:, pl.ds(core, 1)].reshape(HALF, GROUP * HD)


def pack(keys, values, query_keys, query_values, weight, rows):
    return pl.pallas_call(
        pack_kernel,
        out_shape=(pltpu.VMEM((PACKED, HD), BF16), pltpu.VMEM((HALF, GROUP * HD), BF16)),
        in_specs=[IN_VMEM] * 6,
        out_specs=(IN_VMEM, IN_VMEM),
        name="pack",
    )(keys, values, query_keys, query_values, weight, rows.reshape(8, 2, 32, GROUP * HD))


def query_kernel(rows_ref, own_ref, mate_ref, out_ref):
    core, block = position_of()
    mate = block + 1 - 2 * core
    rows = rows_ref[...]
    own_keys, own_values = own_ref[0:BLK, :], own_ref[BLK : 2 * BLK, :]
    mate_keys, mate_values = mate_ref[0:BLK, :], mate_ref[BLK : 2 * BLK, :]
    own_tail, mate_tail = own_ref[TAIL:WEIGHT, :].astype(F32), mate_ref[TAIL:WEIGHT, :].astype(F32)
    tail_keys = jnp.concatenate([own_tail[:SHARE], mate_tail[:SHARE]], 0).astype(BF16)
    tail_values = jnp.concatenate([own_tail[SHARE:], mate_tail[SHARE:]], 0).astype(BF16)

    index = lax.broadcasted_iota(jnp.int32, (HALF, 2 * SHARE), 0)
    position = (index // 32) * 64 + core * 32 + index % 32
    column = lax.broadcasted_iota(jnp.int32, (HALF, 2 * SHARE), 1)
    own_seen = (column < SHARE) & (position >= block * SHARE + column)
    mate_seen = (column >= SHARE) & (position >= mate * SHARE + column - SHARE)

    lane = lax.broadcasted_iota(jnp.int32, (HALF, HD), 1)
    stats = jnp.zeros((HALF, HD), F32)

    def attend(q, keys, values, tail, seen):
        scores = nt(q, keys) * SCALE
        tail = jnp.where(seen, tail, -jnp.inf)
        top = jnp.maximum(
            jnp.max(scores, axis=-1, keepdims=True), jnp.max(tail, axis=-1, keepdims=True)
        )
        weights, tail = jnp.exp(scores - top), jnp.exp(tail - top)
        total = jnp.sum(weights, axis=-1, keepdims=True) + jnp.sum(tail, axis=-1, keepdims=True)
        summed = nn(weights.astype(BF16), values) + nn(tail.astype(BF16), tail_values)
        return top, total, summed

    for h in range(GROUP):
        q = rows[:, h * HD : (h + 1) * HD]
        tail = nt(q, tail_keys) * SCALE
        top0, total0, summed0 = attend(q, own_keys, own_values, tail, own_seen)
        top1, total1, summed1 = attend(q, mate_keys, mate_values, tail, mate_seen)
        top = jnp.maximum(top0, top1)
        factor0, factor1 = jnp.exp(top0 - top), jnp.exp(top1 - top)
        out_ref[:, h * HD : (h + 1) * HD] = (summed0 * factor0 + summed1 * factor1).astype(BF16)
        total = total0 * factor0 + total1 * factor1
        first = top.astype(BF16).astype(F32)
        second = (top - first).astype(BF16).astype(F32)
        high = total.astype(BF16).astype(F32)
        terms = (first, second, top - first - second, high, total - high)
        for i, term in enumerate(terms):
            stats = jnp.where(lane == i * GROUP + h, term, stats)
    out_ref[:, STATS:ANCHOR] = stats.astype(BF16)

    @pl.when(core == 0)
    def _():
        out_ref[:, ANCHOR : ANCHOR + HD] = own_keys
        out_ref[:, ANCHOR + HD : FIRST] = own_values

    @pl.when(core != 0)
    def _():
        out_ref[:, ANCHOR : ANCHOR + HD] = mate_keys
        out_ref[:, ANCHOR + HD : FIRST] = mate_values


def query_parts(rows, own, mate):
    return pl.pallas_call(
        query_kernel,
        out_shape=pltpu.VMEM((HALF, FIRST), BF16),
        in_specs=[IN_VMEM] * 3,
        out_specs=IN_VMEM,
        name="query_parts",
    )(vmem(rows), vmem(own), vmem(mate))


def merge_kernel(parts_ref, out_ref):
    stats = parts_ref[:, :, STATS:ANCHOR].astype(F32)
    flat = stats.reshape(PEERS * SHARE, HD)
    top = flat + (pltpu.roll(flat, HD - GROUP, 1) + pltpu.roll(flat, HD - 2 * GROUP, 1))
    top = top.reshape(PEERS, SHARE, HD)
    factor = jnp.exp(top - jnp.max(top, axis=0, keepdims=True))
    for h in range(GROUP):
        weight = jnp.broadcast_to(factor[:, :, h : h + 1], (PEERS, SHARE, HD))
        totals = jnp.sum(weight * stats, axis=0)
        high, low = 3 * GROUP + h, 4 * GROUP + h
        total = totals[:, high : high + 1] + totals[:, low : low + 1]
        part = parts_ref[:, :, h * HD : (h + 1) * HD].astype(F32)
        attended = (jnp.sum(weight * part, axis=0) / total).astype(BF16)
        out_ref[:, :, h * HD : (h + 1) * HD] = jnp.broadcast_to(attended[None], (PEERS, SHARE, HD))
    anchor = parts_ref[0, :, ANCHOR:FIRST]
    out_ref[:, :, GROUP * HD :] = jnp.broadcast_to(anchor[None], (PEERS, SHARE, 2 * HD))


def merge_parts(parts):
    return pl.pallas_call(
        merge_kernel,
        out_shape=pltpu.VMEM((PEERS, SHARE, SECOND), BF16),
        in_specs=[IN_VMEM],
        out_specs=IN_VMEM,
        name="merge_parts",
    )(vmem(parts))


def project_kernel(rows_ref, own_ref, mate_ref, out_ref):
    core, unused = position_of()
    rows = rows_ref[:, :, : GROUP * HD].astype(F32).reshape(8, 2, 16, GROUP * HD)
    upper = rows[:, 0].reshape(128, GROUP * HD).astype(BF16)
    lower = rows[:, 1].reshape(128, GROUP * HD).astype(BF16)

    def packed(ref):
        pieces = [ref[WEIGHT + h * 64 : WEIGHT + (h + 1) * 64, :] for h in range(GROUP)]
        weight = jnp.concatenate(pieces, 1)
        zero = jnp.zeros_like(weight)
        left = jnp.concatenate([weight, zero], 0)
        right = jnp.concatenate([zero, weight], 0)
        return (nt(upper, left) + nt(lower, right)).reshape(8, 16, 128)

    out_ref[pl.ds(core, 1)] = packed(own_ref)[None]
    out_ref[pl.ds(1 - core, 1)] = packed(mate_ref)[None]


def project(rows, own, mate):
    return pl.pallas_call(
        project_kernel,
        out_shape=pltpu.VMEM((2, 8, 16, 128), F32),
        in_specs=[IN_VMEM] * 3,
        out_specs=IN_VMEM,
        name="project",
    )(vmem(rows), vmem(own), vmem(mate))


def context_kernel(q_ref, keys_ref, values_ref, anchor_ref, out_ref):
    has_anchor = position_of()[1] > 0
    anchor = anchor_ref[:, :, GROUP * HD :].astype(F32).reshape(BLK, 2 * HD).astype(BF16)
    anchor_keys, anchor_values = anchor[:, :HD], anchor[:, HD:]
    keys, values = keys_ref[...], values_ref[...]
    row = lax.broadcasted_iota(jnp.int32, (BLK, BLK), 0)
    column = lax.broadcasted_iota(jnp.int32, (BLK, BLK), 1)
    for h in range(GROUP):
        q = q_ref[:, h * HD : (h + 1) * HD]
        own = jnp.where(row >= column, nt(q, keys) * SCALE, -jnp.inf)
        first = jnp.where(has_anchor, nt(q, anchor_keys) * SCALE, -jnp.inf)
        top = jnp.max(jnp.maximum(own, first), axis=-1, keepdims=True)
        own, first = jnp.exp(own - top), jnp.exp(first - top)
        total = jnp.sum(own + first, axis=-1, keepdims=True)
        summed = nn(own.astype(BF16), values) + nn(first.astype(BF16), anchor_values)
        out_ref[:, h * HD : (h + 1) * HD] = (summed / total).astype(BF16)


def context(queries, keys, values, gathered):
    return pl.pallas_call(
        context_kernel,
        out_shape=jax.ShapeDtypeStruct((BLK, GROUP * HD), BF16),
        in_specs=[IN_VMEM] * 4,
        cost_estimate=pl.CostEstimate(
            flops=4 * BLK * GROUP * 2 * BLK * HD,
            transcendentals=BLK * GROUP * 2 * BLK,
            bytes_accessed=1 << 20,
        ),
        name="context",
    )(queries, keys, values, vmem(gathered))


def finish_kernel(parts_ref, out_ref):
    for k in range(2):
        summed = jnp.sum(parts_ref[k * 8 : (k + 1) * 8], axis=0)
        out_ref[k * 32 : k * 32 + 16, :] = summed[:, :64].astype(BF16)
        out_ref[k * 32 + 16 : k * 32 + 32, :] = summed[:, 64:].astype(BF16)


def finish(parts):
    return pl.pallas_call(
        finish_kernel,
        out_shape=jax.ShapeDtypeStruct((64, 64), BF16),
        in_specs=[IN_VMEM],
        name="finish",
    )(vmem(parts))


def body(ctx_queries, ctx_keys, ctx_values, query_queries, query_keys, query_values, out_weight):
    own, rows = pack(ctx_keys, ctx_values, query_keys, query_values, out_weight.T, query_queries)
    mate = lax.ppermute(own, "core", [(0, 1), (1, 0)])

    parts = query_parts(rows, own, mate)
    parts = lax.all_to_all(parts.reshape(PEERS, SHARE, FIRST), ("z", "x"), 0, 0)
    message = merge_parts(parts)
    gathered = lax.all_to_all(message, ("z", "x"), 0, 0)

    sums = project(gathered, own, mate)
    sums = lax.all_to_all(sums.reshape(16, 16, 128), ("core", "tp"), 0, 0)
    ctx_out = context(ctx_queries, ctx_keys, ctx_values, gathered)
    query_out = finish(sums)
    return (ctx_out, query_out)


def solution(mesh):
    fine = Mesh(mesh.devices.reshape(8, 4, 2, 8), ("z", "x", "core", "tp"))
    ctx = ("z", "x", "core")
    return jax.shard_map(
        body,
        mesh=fine,
        in_specs=(
            P(ctx, "tp"),
            P(ctx, "tp"),
            P(ctx, "tp"),
            P(None, "tp"),
            P(ctx, "tp"),
            P(ctx, "tp"),
            P("tp", ctx),
        ),
        out_specs=(P(ctx, "tp"), P("tp", ctx)),
        check_vma=False,
    )
```

```python
import jax
import jax.numpy as jnp
from jax import lax
from jax.experimental import pallas as pl
from jax.experimental.pallas import tpu as pltpu
from jax.sharding import Mesh
from jax.sharding import PartitionSpec as P

HD = 128
GROUP = 4
BLK = 256
QL = 512
SHARE = 8
PEERS = 32
HALF = QL // 2
SCALE = HD**-0.5
F32 = jnp.float32
BF16 = jnp.bfloat16

STATS = GROUP * HD
ANCHOR = STATS + HD
FIRST = ANCHOR + 2 * HD
SECOND = GROUP * HD + 2 * HD


TAIL = 2 * BLK
WEIGHT = TAIL + 2 * SHARE
PACKED = WEIGHT + GROUP * 64


def nt(a, b):
    return lax.dot_general(a, b, (((1,), (1,)), ((), ())), preferred_element_type=F32)


def nn(a, b):
    return lax.dot_general(a, b, (((1,), (0,)), ((), ())), preferred_element_type=F32)


def vmem(array):
    return pltpu.with_memory_space_constraint(array, pltpu.VMEM)


IN_VMEM = pl.BlockSpec(memory_space=pltpu.VMEM)


def position_of():
    core = lax.axis_index("core")
    return core, (lax.axis_index("z") * 4 + lax.axis_index("x")) * 2 + core


def pack_kernel(
    keys_ref, values_ref, query_keys_ref, query_values_ref, weight_ref, rows_ref, out_ref, half_ref
):
    out_ref[0:BLK, :] = keys_ref[...]
    out_ref[BLK : 2 * BLK, :] = values_ref[...]
    tail = jnp.concatenate([query_keys_ref[...].astype(F32), query_values_ref[...].astype(F32)], 0)
    out_ref[TAIL:WEIGHT, :] = tail.astype(BF16)
    for h in range(GROUP):
        start = WEIGHT + h * 64
        out_ref[start : start + 64, :] = weight_ref[:, h * HD : (h + 1) * HD]
    core, unused = position_of()
    half_ref[...] = rows_ref[:, pl.ds(core, 1)].reshape(HALF, GROUP * HD)


def pack(keys, values, query_keys, query_values, weight, rows):
    return pl.pallas_call(
        pack_kernel,
        out_shape=(pltpu.VMEM((PACKED, HD), BF16), pltpu.VMEM((HALF, GROUP * HD), BF16)),
        in_specs=[IN_VMEM] * 6,
        out_specs=(IN_VMEM, IN_VMEM),
        name="pack",
    )(keys, values, query_keys, query_values, weight, rows.reshape(8, 2, 32, GROUP * HD))


def query_kernel(rows_ref, own_ref, mate_ref, out_ref):
    core, block = position_of()
    mate = block + 1 - 2 * core
    rows = rows_ref[...]
    own_keys, own_values = own_ref[0:BLK, :], own_ref[BLK : 2 * BLK, :]
    mate_keys, mate_values = mate_ref[0:BLK, :], mate_ref[BLK : 2 * BLK, :]
    own_tail, mate_tail = own_ref[TAIL:WEIGHT, :].astype(F32), mate_ref[TAIL:WEIGHT, :].astype(F32)
    tail_keys = jnp.concatenate([own_tail[:SHARE], mate_tail[:SHARE]], 0).astype(BF16)
    tail_values = jnp.concatenate([own_tail[SHARE:], mate_tail[SHARE:]], 0).astype(BF16)

    index = lax.broadcasted_iota(jnp.int32, (HALF, 2 * SHARE), 0)
    position = (index // 32) * 64 + core * 32 + index % 32
    column = lax.broadcasted_iota(jnp.int32, (HALF, 2 * SHARE), 1)
    own_seen = (column < SHARE) & (position >= block * SHARE + column)
    mate_seen = (column >= SHARE) & (position >= mate * SHARE + column - SHARE)

    lane = lax.broadcasted_iota(jnp.int32, (HALF, HD), 1)
    stats = jnp.zeros((HALF, HD), F32)

    def attend(q, keys, values, tail, seen):
        scores = nt(q, keys) * SCALE
        tail = jnp.where(seen, tail, -jnp.inf)
        top = jnp.maximum(
            jnp.max(scores, axis=-1, keepdims=True), jnp.max(tail, axis=-1, keepdims=True)
        )
        weights, tail = jnp.exp(scores - top), jnp.exp(tail - top)
        total = jnp.sum(weights, axis=-1, keepdims=True) + jnp.sum(tail, axis=-1, keepdims=True)
        summed = nn(weights.astype(BF16), values) + nn(tail.astype(BF16), tail_values)
        return top, total, summed

    for h in range(GROUP):
        q = rows[:, h * HD : (h + 1) * HD]
        tail = nt(q, tail_keys) * SCALE
        top0, total0, summed0 = attend(q, own_keys, own_values, tail, own_seen)
        top1, total1, summed1 = attend(q, mate_keys, mate_values, tail, mate_seen)
        top = jnp.maximum(top0, top1)
        factor0, factor1 = jnp.exp(top0 - top), jnp.exp(top1 - top)
        out_ref[:, h * HD : (h + 1) * HD] = (summed0 * factor0 + summed1 * factor1).astype(BF16)
        total = total0 * factor0 + total1 * factor1
        first = top.astype(BF16).astype(F32)
        second = (top - first).astype(BF16).astype(F32)
        high = total.astype(BF16).astype(F32)
        terms = (first, second, top - first - second, high, total - high)
        for i, term in enumerate(terms):
            stats = jnp.where(lane == i * GROUP + h, term, stats)
    out_ref[:, STATS:ANCHOR] = stats.astype(BF16)

    @pl.when(core == 0)
    def _():
        out_ref[:, ANCHOR : ANCHOR + HD] = own_keys
        out_ref[:, ANCHOR + HD : FIRST] = own_values

    @pl.when(core != 0)
    def _():
        out_ref[:, ANCHOR : ANCHOR + HD] = mate_keys
        out_ref[:, ANCHOR + HD : FIRST] = mate_values


def query_parts(rows, own, mate):
    return pl.pallas_call(
        query_kernel,
        out_shape=pltpu.VMEM((HALF, FIRST), BF16),
        in_specs=[IN_VMEM] * 3,
        out_specs=IN_VMEM,
        name="query_parts",
    )(vmem(rows), vmem(own), vmem(mate))


def merge_kernel(parts_ref, out_ref):
    stats = parts_ref[:, :, STATS:ANCHOR].astype(F32)
    flat = stats.reshape(PEERS * SHARE, HD)
    top = flat + (pltpu.roll(flat, HD - GROUP, 1) + pltpu.roll(flat, HD - 2 * GROUP, 1))
    top = top.reshape(PEERS, SHARE, HD)
    factor = jnp.exp(top - jnp.max(top, axis=0, keepdims=True))
    for h in range(GROUP):
        weight = jnp.broadcast_to(factor[:, :, h : h + 1], (PEERS, SHARE, HD))
        totals = jnp.sum(weight * stats, axis=0)
        high, low = 3 * GROUP + h, 4 * GROUP + h
        total = totals[:, high : high + 1] + totals[:, low : low + 1]
        part = parts_ref[:, :, h * HD : (h + 1) * HD].astype(F32)
        attended = (jnp.sum(weight * part, axis=0) / total).astype(BF16)
        out_ref[:, :, h * HD : (h + 1) * HD] = jnp.broadcast_to(attended[None], (PEERS, SHARE, HD))
    anchor = parts_ref[0, :, ANCHOR:FIRST]
    out_ref[:, :, GROUP * HD :] = jnp.broadcast_to(anchor[None], (PEERS, SHARE, 2 * HD))


def merge_parts(parts):
    return pl.pallas_call(
        merge_kernel,
        out_shape=pltpu.VMEM((PEERS, SHARE, SECOND), BF16),
        in_specs=[IN_VMEM],
        out_specs=IN_VMEM,
        name="merge_parts",
    )(vmem(parts))


def tail_kernel(gathered_ref, own_ref, mate_ref, q_ref, sums_ref, out_ref):
    core, block = position_of()
    rows = gathered_ref[:, :, : GROUP * HD].astype(F32).reshape(8, 2, 16, GROUP * HD)
    upper = rows[:, 0].reshape(128, GROUP * HD).astype(BF16)
    lower = rows[:, 1].reshape(128, GROUP * HD).astype(BF16)

    def packed(ref):
        pieces = [ref[WEIGHT + h * 64 : WEIGHT + (h + 1) * 64, :] for h in range(GROUP)]
        weight = jnp.concatenate(pieces, 1)
        zero = jnp.zeros_like(weight)
        left = jnp.concatenate([weight, zero], 0)
        right = jnp.concatenate([zero, weight], 0)
        return (nt(upper, left) + nt(lower, right)).reshape(8, 16, 128)

    sums_ref[pl.ds(core, 1)] = packed(own_ref)[None]
    sums_ref[pl.ds(1 - core, 1)] = packed(mate_ref)[None]

    has_anchor = block > 0
    anchor = gathered_ref[:, :, GROUP * HD :].astype(F32).reshape(BLK, 2 * HD).astype(BF16)
    anchor_keys, anchor_values = anchor[:, :HD], anchor[:, HD:]
    keys, values = own_ref[0:BLK, :], own_ref[BLK : 2 * BLK, :]
    row = lax.broadcasted_iota(jnp.int32, (BLK, BLK), 0)
    column = lax.broadcasted_iota(jnp.int32, (BLK, BLK), 1)
    for h in range(GROUP):
        q = q_ref[:, h * HD : (h + 1) * HD]
        own = jnp.where(row >= column, nt(q, keys) * SCALE, -jnp.inf)
        first = jnp.where(has_anchor, nt(q, anchor_keys) * SCALE, -jnp.inf)
        top = jnp.max(jnp.maximum(own, first), axis=-1, keepdims=True)
        own, first = jnp.exp(own - top), jnp.exp(first - top)
        total = jnp.sum(own + first, axis=-1, keepdims=True)
        summed = nn(own.astype(BF16), values) + nn(first.astype(BF16), anchor_values)
        out_ref[:, h * HD : (h + 1) * HD] = (summed / total).astype(BF16)


def project_and_attend(gathered, own, mate, queries):
    return pl.pallas_call(
        tail_kernel,
        out_shape=(
            pltpu.VMEM((2, 8, 16, 128), F32),
            jax.ShapeDtypeStruct((BLK, GROUP * HD), BF16),
        ),
        in_specs=[IN_VMEM] * 4,
        out_specs=(IN_VMEM, IN_VMEM),
        name="project_and_attend",
    )(vmem(gathered), vmem(own), vmem(mate), vmem(queries))


def finish_kernel(parts_ref, out_ref):
    for k in range(2):
        summed = jnp.sum(parts_ref[k * 8 : (k + 1) * 8], axis=0)
        out_ref[k * 32 : k * 32 + 16, :] = summed[:, :64].astype(BF16)
        out_ref[k * 32 + 16 : k * 32 + 32, :] = summed[:, 64:].astype(BF16)


def finish(parts):
    return pl.pallas_call(
        finish_kernel,
        out_shape=jax.ShapeDtypeStruct((64, 64), BF16),
        in_specs=[IN_VMEM],
        name="finish",
    )(vmem(parts))


def body(ctx_queries, ctx_keys, ctx_values, query_queries, query_keys, query_values, out_weight):
    own, rows = pack(ctx_keys, ctx_values, query_keys, query_values, out_weight.T, query_queries)
    mate = lax.ppermute(own, "core", [(0, 1), (1, 0)])

    parts = query_parts(rows, own, mate)
    parts = lax.all_to_all(parts.reshape(PEERS, SHARE, FIRST), ("z", "x"), 0, 0)
    message = merge_parts(parts)
    gathered = lax.all_to_all(message, ("z", "x"), 0, 0)

    sums, ctx_out = project_and_attend(gathered, own, mate, ctx_queries)
    sums = lax.all_to_all(sums.reshape(16, 16, 128), ("core", "tp"), 0, 0)
    query_out = finish(sums)
    return (ctx_out, query_out)


def solution(mesh):
    fine = Mesh(mesh.devices.reshape(8, 4, 2, 8), ("z", "x", "core", "tp"))
    ctx = ("z", "x", "core")
    return jax.shard_map(
        body,
        mesh=fine,
        in_specs=(
            P(ctx, "tp"),
            P(ctx, "tp"),
            P(ctx, "tp"),
            P(None, "tp"),
            P(ctx, "tp"),
            P(ctx, "tp"),
            P("tp", ctx),
        ),
        out_specs=(P(ctx, "tp"), P("tp", ctx)),
        check_vma=False,
    )
```

```python
import jax
import jax.numpy as jnp
from jax import lax
from jax.experimental import pallas as pl
from jax.experimental.pallas import tpu as pltpu
from jax.sharding import Mesh
from jax.sharding import PartitionSpec as P

HD = 128
GROUP = 4
BLK = 256
QL = 512
SHARE = 8
PEERS = 32
HALF = QL // 2
SCALE = HD**-0.5
F32 = jnp.float32
BF16 = jnp.bfloat16

STATS = GROUP * HD
ANCHOR = STATS + HD
FIRST = ANCHOR + HD
SECOND = GROUP * HD + 2 * HD
TAIL = 2 * BLK
WEIGHT = TAIL + 2 * SHARE
PACKED = WEIGHT + GROUP * 64


def nt(a, b):
    return lax.dot_general(a, b, (((1,), (1,)), ((), ())), preferred_element_type=F32)


def nn(a, b):
    return lax.dot_general(a, b, (((1,), (0,)), ((), ())), preferred_element_type=F32)


def vmem(array):
    return pltpu.with_memory_space_constraint(array, pltpu.VMEM)


IN_VMEM = pl.BlockSpec(memory_space=pltpu.VMEM)


def position_of():
    core = lax.axis_index("core")
    return core, (lax.axis_index("z") * 4 + lax.axis_index("x")) * 2 + core


def pack_kernel(
    keys_ref, values_ref, query_keys_ref, query_values_ref, weight_ref, rows_ref, out_ref, half_ref
):
    out_ref[0:BLK, :] = keys_ref[...]
    out_ref[BLK : 2 * BLK, :] = values_ref[...]
    tail = jnp.concatenate([query_keys_ref[...].astype(F32), query_values_ref[...].astype(F32)], 0)
    out_ref[TAIL:WEIGHT, :] = tail.astype(BF16)
    for h in range(GROUP):
        start = WEIGHT + h * 64
        out_ref[start : start + 64, :] = weight_ref[:, h * HD : (h + 1) * HD]
    core, unused = position_of()
    half_ref[...] = rows_ref[:, pl.ds(core, 1)].reshape(HALF, GROUP * HD)


def pack(keys, values, query_keys, query_values, weight, rows):
    return pl.pallas_call(
        pack_kernel,
        out_shape=(pltpu.VMEM((PACKED, HD), BF16), pltpu.VMEM((HALF, GROUP * HD), BF16)),
        in_specs=[IN_VMEM] * 6,
        out_specs=(IN_VMEM, IN_VMEM),
        name="pack",
    )(keys, values, query_keys, query_values, weight, rows.reshape(8, 2, 32, GROUP * HD))


def query_kernel(rows_ref, own_ref, mate_ref, out_ref):
    core, block = position_of()
    mate = block + 1 - 2 * core
    rows = rows_ref[...]
    own_keys, own_values = own_ref[0:BLK, :], own_ref[BLK : 2 * BLK, :]
    mate_keys, mate_values = mate_ref[0:BLK, :], mate_ref[BLK : 2 * BLK, :]
    own_tail, mate_tail = own_ref[TAIL:WEIGHT, :].astype(F32), mate_ref[TAIL:WEIGHT, :].astype(F32)
    tail_keys = jnp.concatenate([own_tail[:SHARE], mate_tail[:SHARE]], 0).astype(BF16)
    tail_values = jnp.concatenate([own_tail[SHARE:], mate_tail[SHARE:]], 0).astype(BF16)

    index = lax.broadcasted_iota(jnp.int32, (HALF, 2 * SHARE), 0)
    position = (index // 32) * 64 + core * 32 + index % 32
    column = lax.broadcasted_iota(jnp.int32, (HALF, 2 * SHARE), 1)
    own_seen = (column < SHARE) & (position >= block * SHARE + column)
    mate_seen = (column >= SHARE) & (position >= mate * SHARE + column - SHARE)

    lane = lax.broadcasted_iota(jnp.int32, (HALF, HD), 1)
    stats = jnp.zeros((HALF, HD), F32)

    def attend(q, keys, values, tail, seen):
        scores = nt(q, keys) * SCALE
        tail = jnp.where(seen, tail, -jnp.inf)
        top = jnp.maximum(
            jnp.max(scores, axis=-1, keepdims=True), jnp.max(tail, axis=-1, keepdims=True)
        )
        weights, tail = jnp.exp(scores - top), jnp.exp(tail - top)
        total = jnp.sum(weights, axis=-1, keepdims=True) + jnp.sum(tail, axis=-1, keepdims=True)
        summed = nn(weights.astype(BF16), values) + nn(tail.astype(BF16), tail_values)
        return top, total, summed

    for h in range(GROUP):
        q = rows[:, h * HD : (h + 1) * HD]
        tail = nt(q, tail_keys) * SCALE
        top0, total0, summed0 = attend(q, own_keys, own_values, tail, own_seen)
        top1, total1, summed1 = attend(q, mate_keys, mate_values, tail, mate_seen)
        top = jnp.maximum(top0, top1)
        factor0, factor1 = jnp.exp(top0 - top), jnp.exp(top1 - top)
        out_ref[:, h * HD : (h + 1) * HD] = (summed0 * factor0 + summed1 * factor1).astype(BF16)
        total = total0 * factor0 + total1 * factor1
        first = top.astype(BF16).astype(F32)
        second = (top - first).astype(BF16).astype(F32)
        high = total.astype(BF16).astype(F32)
        terms = (first, second, top - first - second, high, total - high)
        for i, term in enumerate(terms):
            stats = jnp.where(lane == i * GROUP + h, term, stats)
    out_ref[:, STATS:ANCHOR] = stats.astype(BF16)

    @pl.when(core == 0)
    def _():
        out_ref[:, ANCHOR:FIRST] = own_keys

    @pl.when(core != 0)
    def _():
        out_ref[:, ANCHOR:FIRST] = mate_values


def query_parts(rows, own, mate):
    return pl.pallas_call(
        query_kernel,
        out_shape=pltpu.VMEM((HALF, FIRST), BF16),
        in_specs=[IN_VMEM] * 3,
        out_specs=IN_VMEM,
        name="query_parts",
    )(vmem(rows), vmem(own), vmem(mate))


def merge_kernel(parts_ref, out_ref):
    stats = parts_ref[:, :, STATS:ANCHOR].astype(F32)
    flat = stats.reshape(PEERS * SHARE, HD)
    top = flat + (pltpu.roll(flat, HD - GROUP, 1) + pltpu.roll(flat, HD - 2 * GROUP, 1))
    top = top.reshape(PEERS, SHARE, HD)
    factor = jnp.exp(top - jnp.max(top, axis=0, keepdims=True))
    for h in range(GROUP):
        weight = jnp.broadcast_to(factor[:, :, h : h + 1], (PEERS, SHARE, HD))
        totals = jnp.sum(weight * stats, axis=0)
        high, low = 3 * GROUP + h, 4 * GROUP + h
        total = totals[:, high : high + 1] + totals[:, low : low + 1]
        part = parts_ref[:, :, h * HD : (h + 1) * HD].astype(F32)
        attended = (jnp.sum(weight * part, axis=0) / total).astype(BF16)
        out_ref[:, :, h * HD : (h + 1) * HD] = jnp.broadcast_to(attended[None], (PEERS, SHARE, HD))
    anchor = jnp.broadcast_to(parts_ref[0, :, ANCHOR:FIRST][None], (PEERS, SHARE, HD))
    out_ref[:, :, GROUP * HD : (GROUP + 1) * HD] = anchor
    out_ref[:, :, (GROUP + 1) * HD :] = anchor


def merge_parts(parts):
    return pl.pallas_call(
        merge_kernel,
        out_shape=pltpu.VMEM((PEERS, SHARE, SECOND), BF16),
        in_specs=[IN_VMEM],
        out_specs=IN_VMEM,
        name="merge_parts",
    )(vmem(parts))


def project_kernel(rows_ref, own_ref, mate_ref, out_ref, half_ref):
    core, unused = position_of()
    rows = rows_ref[:, :, : GROUP * HD].astype(F32).reshape(8, 2, 16, GROUP * HD)
    upper = rows[:, 0].reshape(128, GROUP * HD).astype(BF16)
    lower = rows[:, 1].reshape(128, GROUP * HD).astype(BF16)

    def packed(ref):
        pieces = [ref[WEIGHT + h * 64 : WEIGHT + (h + 1) * 64, :] for h in range(GROUP)]
        weight = jnp.concatenate(pieces, 1)
        zero = jnp.zeros_like(weight)
        left = jnp.concatenate([weight, zero], 0)
        right = jnp.concatenate([zero, weight], 0)
        return (nt(upper, left) + nt(lower, right)).reshape(8, 16, 128)

    out_ref[pl.ds(core, 1)] = packed(own_ref)[None]
    out_ref[pl.ds(1 - core, 1)] = packed(mate_ref)[None]
    half = rows_ref[:, :, GROUP * HD : (GROUP + 1) * HD].astype(F32)
    half_ref[...] = half.reshape(BLK, HD).astype(BF16)


def project(rows, own, mate):
    return pl.pallas_call(
        project_kernel,
        out_shape=(pltpu.VMEM((2, 8, 16, 128), F32), pltpu.VMEM((BLK, HD), BF16)),
        in_specs=[IN_VMEM] * 3,
        out_specs=(IN_VMEM, IN_VMEM),
        name="project",
    )(vmem(rows), vmem(own), vmem(mate))


def context_kernel(q_ref, own_ref, half_ref, other_ref, out_ref):
    core, block = position_of()
    has_anchor = block > 0
    half, other = half_ref[...].astype(F32), other_ref[...].astype(F32)
    anchor_keys = jnp.where(core == 0, half, other).astype(BF16)
    anchor_values = jnp.where(core == 0, other, half).astype(BF16)
    keys, values = own_ref[0:BLK, :], own_ref[BLK : 2 * BLK, :]
    row = lax.broadcasted_iota(jnp.int32, (BLK, BLK), 0)
    column = lax.broadcasted_iota(jnp.int32, (BLK, BLK), 1)
    for h in range(GROUP):
        q = q_ref[:, h * HD : (h + 1) * HD]
        own = jnp.where(row >= column, nt(q, keys) * SCALE, -jnp.inf)
        first = jnp.where(has_anchor, nt(q, anchor_keys) * SCALE, -jnp.inf)
        top = jnp.max(jnp.maximum(own, first), axis=-1, keepdims=True)
        own, first = jnp.exp(own - top), jnp.exp(first - top)
        total = jnp.sum(own + first, axis=-1, keepdims=True)
        summed = nn(own.astype(BF16), values) + nn(first.astype(BF16), anchor_values)
        out_ref[:, h * HD : (h + 1) * HD] = (summed / total).astype(BF16)


def context(queries, own, half, other):
    return pl.pallas_call(
        context_kernel,
        out_shape=jax.ShapeDtypeStruct((BLK, GROUP * HD), BF16),
        in_specs=[IN_VMEM] * 4,
        cost_estimate=pl.CostEstimate(
            flops=4 * BLK * GROUP * 2 * BLK * HD,
            transcendentals=BLK * GROUP * 2 * BLK,
            bytes_accessed=1 << 20,
        ),
        name="context",
    )(vmem(queries), vmem(own), vmem(half), vmem(other))


def finish_kernel(parts_ref, out_ref):
    for k in range(2):
        summed = jnp.sum(parts_ref[k * 8 : (k + 1) * 8], axis=0)
        out_ref[k * 32 : k * 32 + 16, :] = summed[:, :64].astype(BF16)
        out_ref[k * 32 + 16 : k * 32 + 32, :] = summed[:, 64:].astype(BF16)


def finish(parts):
    return pl.pallas_call(
        finish_kernel,
        out_shape=jax.ShapeDtypeStruct((64, 64), BF16),
        in_specs=[IN_VMEM],
        name="finish",
    )(vmem(parts))


def body(ctx_queries, ctx_keys, ctx_values, query_queries, query_keys, query_values, out_weight):
    own, rows = pack(ctx_keys, ctx_values, query_keys, query_values, out_weight.T, query_queries)
    mate = lax.ppermute(own, "core", [(0, 1), (1, 0)])

    parts = query_parts(rows, own, mate)
    parts = lax.all_to_all(parts.reshape(PEERS, SHARE, FIRST), ("z", "x"), 0, 0)
    message = merge_parts(parts)
    gathered = lax.all_to_all(message, ("z", "x"), 0, 0)

    sums, half = project(gathered, own, mate)
    sums = lax.all_to_all(sums.reshape(16, 16, 128), ("core", "tp"), 0, 0)
    other = lax.ppermute(half, "core", [(0, 1), (1, 0)])
    ctx_out = context(ctx_queries, own, half, other)
    query_out = finish(sums)
    return (ctx_out, query_out)


def solution(mesh):
    fine = Mesh(mesh.devices.reshape(8, 4, 2, 8), ("z", "x", "core", "tp"))
    ctx = ("z", "x", "core")
    return jax.shard_map(
        body,
        mesh=fine,
        in_specs=(
            P(ctx, "tp"),
            P(ctx, "tp"),
            P(ctx, "tp"),
            P(None, "tp"),
            P(ctx, "tp"),
            P(ctx, "tp"),
            P("tp", ctx),
        ),
        out_specs=(P(ctx, "tp"), P("tp", ctx)),
        check_vma=False,
    )
```

```python
import jax
import jax.numpy as jnp
from jax import lax
from jax.experimental import pallas as pl
from jax.experimental.pallas import tpu as pltpu
from jax.sharding import Mesh
from jax.sharding import PartitionSpec as P

HD = 128
GROUP = 4
BLK = 256
QL = 512
SHARE = 8
PEERS = 32
HALF = QL // 2
SCALE = HD**-0.5
F32 = jnp.float32
BF16 = jnp.bfloat16

STATS = GROUP * HD
ANCHOR = STATS + HD
FIRST = ANCHOR + HD
SECOND = GROUP * HD + 2 * HD
TAIL = 2 * BLK
WEIGHT = TAIL + 2 * SHARE
PACKED = WEIGHT + GROUP * 64


def nt(a, b):
    return lax.dot_general(a, b, (((1,), (1,)), ((), ())), preferred_element_type=F32)


def nn(a, b):
    return lax.dot_general(a, b, (((1,), (0,)), ((), ())), preferred_element_type=F32)


def vmem(array):
    return pltpu.with_memory_space_constraint(array, pltpu.VMEM)


IN_VMEM = pl.BlockSpec(memory_space=pltpu.VMEM)


def position_of():
    core = lax.axis_index("core")
    return core, (lax.axis_index("z") * 4 + lax.axis_index("x")) * 2 + core


def pack_kernel(
    keys_ref, values_ref, query_keys_ref, query_values_ref, weight_ref, rows_ref, out_ref, half_ref
):
    out_ref[0:BLK, :] = keys_ref[...]
    out_ref[BLK : 2 * BLK, :] = values_ref[...]
    tail = jnp.concatenate([query_keys_ref[...].astype(F32), query_values_ref[...].astype(F32)], 0)
    out_ref[TAIL:WEIGHT, :] = tail.astype(BF16)
    for h in range(GROUP):
        start = WEIGHT + h * 64
        out_ref[start : start + 64, :] = weight_ref[:, h * HD : (h + 1) * HD]
    core, unused = position_of()
    half_ref[...] = rows_ref[:, pl.ds(core, 1)].reshape(HALF, GROUP * HD)


def pack(keys, values, query_keys, query_values, weight, rows):
    return pl.pallas_call(
        pack_kernel,
        out_shape=(pltpu.VMEM((PACKED, HD), BF16), pltpu.VMEM((HALF, GROUP * HD), BF16)),
        in_specs=[IN_VMEM] * 6,
        out_specs=(IN_VMEM, IN_VMEM),
        name="pack",
    )(keys, values, query_keys, query_values, weight, rows.reshape(8, 2, 32, GROUP * HD))


def attend_block(rows_ref, pack_ref, core, block):
    rows = rows_ref[...]
    keys, values = pack_ref[0:BLK, :], pack_ref[BLK : 2 * BLK, :]
    tail_keys = pack_ref[TAIL:WEIGHT, :]
    tail = tail_keys.astype(F32)
    tail_values = jnp.concatenate([tail[SHARE:], tail[:SHARE]], 0).astype(BF16)
    index = lax.broadcasted_iota(jnp.int32, (HALF, 2 * SHARE), 0)
    position = (index // 32) * 64 + core * 32 + index % 32
    column = lax.broadcasted_iota(jnp.int32, (HALF, 2 * SHARE), 1)
    seen = (column < SHARE) & (position >= block * SHARE + column)
    parts = []
    for h in range(GROUP):
        q = rows[:, h * HD : (h + 1) * HD]
        scores = nt(q, keys) * SCALE
        last = jnp.where(seen, nt(q, tail_keys) * SCALE, -jnp.inf)
        top = jnp.maximum(
            jnp.max(scores, axis=-1, keepdims=True), jnp.max(last, axis=-1, keepdims=True)
        )
        weights, last = jnp.exp(scores - top), jnp.exp(last - top)
        total = jnp.sum(weights, axis=-1, keepdims=True) + jnp.sum(last, axis=-1, keepdims=True)
        parts.append((top, total, nn(weights.astype(BF16), values) + nn(last.astype(BF16), tail_values)))
    return parts


def own_kernel(rows_ref, own_ref, summed_ref, stats_ref):
    core, block = position_of()
    lane = lax.broadcasted_iota(jnp.int32, (HALF, HD), 1)
    stats = jnp.zeros((HALF, HD), F32)
    for h, (top, total, summed) in enumerate(attend_block(rows_ref, own_ref, core, block)):
        summed_ref[:, h * HD : (h + 1) * HD] = summed
        stats = jnp.where(lane == h, top, jnp.where(lane == GROUP + h, total, stats))
    stats_ref[...] = stats


def query_own(rows, own):
    return pl.pallas_call(
        own_kernel,
        out_shape=(pltpu.VMEM((HALF, GROUP * HD), F32), pltpu.VMEM((HALF, HD), F32)),
        in_specs=[IN_VMEM] * 2,
        out_specs=(IN_VMEM, IN_VMEM),
        name="query_own",
    )(vmem(rows), vmem(own))


def mate_kernel(rows_ref, own_ref, mate_ref, summed_ref, stats_ref, out_ref):
    core, block = position_of()
    mate = block + 1 - 2 * core
    lane = lax.broadcasted_iota(jnp.int32, (HALF, HD), 1)
    stats = jnp.zeros((HALF, HD), F32)
    before = stats_ref[...]
    for h, (top1, total1, summed1) in enumerate(attend_block(rows_ref, mate_ref, core, mate)):
        top0, total0 = before[:, h : h + 1], before[:, GROUP + h : GROUP + h + 1]
        summed0 = summed_ref[:, h * HD : (h + 1) * HD]
        top = jnp.maximum(top0, top1)
        factor0, factor1 = jnp.exp(top0 - top), jnp.exp(top1 - top)
        out_ref[:, h * HD : (h + 1) * HD] = (summed0 * factor0 + summed1 * factor1).astype(BF16)
        total = total0 * factor0 + total1 * factor1
        first = top.astype(BF16).astype(F32)
        second = (top - first).astype(BF16).astype(F32)
        high = total.astype(BF16).astype(F32)
        terms = (first, second, top - first - second, high, total - high)
        for i, term in enumerate(terms):
            stats = jnp.where(lane == i * GROUP + h, term, stats)
    out_ref[:, STATS:ANCHOR] = stats.astype(BF16)

    @pl.when(core == 0)
    def _():
        out_ref[:, ANCHOR:FIRST] = own_ref[0:BLK, :]

    @pl.when(core != 0)
    def _():
        out_ref[:, ANCHOR:FIRST] = mate_ref[BLK : 2 * BLK, :]


def query_parts(rows, own, mate, summed, stats):
    return pl.pallas_call(
        mate_kernel,
        out_shape=pltpu.VMEM((HALF, FIRST), BF16),
        in_specs=[IN_VMEM] * 5,
        out_specs=IN_VMEM,
        name="query_parts",
    )(vmem(rows), vmem(own), vmem(mate), vmem(summed), vmem(stats))


def merge_kernel(parts_ref, out_ref):
    stats = parts_ref[:, :, STATS:ANCHOR].astype(F32)
    flat = stats.reshape(PEERS * SHARE, HD)
    top = flat + (pltpu.roll(flat, HD - GROUP, 1) + pltpu.roll(flat, HD - 2 * GROUP, 1))
    top = top.reshape(PEERS, SHARE, HD)
    factor = jnp.exp(top - jnp.max(top, axis=0, keepdims=True))
    for h in range(GROUP):
        weight = jnp.broadcast_to(factor[:, :, h : h + 1], (PEERS, SHARE, HD))
        totals = jnp.sum(weight * stats, axis=0)
        high, low = 3 * GROUP + h, 4 * GROUP + h
        total = totals[:, high : high + 1] + totals[:, low : low + 1]
        part = parts_ref[:, :, h * HD : (h + 1) * HD].astype(F32)
        attended = (jnp.sum(weight * part, axis=0) / total).astype(BF16)
        out_ref[:, :, h * HD : (h + 1) * HD] = jnp.broadcast_to(attended[None], (PEERS, SHARE, HD))
    anchor = jnp.broadcast_to(parts_ref[0, :, ANCHOR:FIRST][None], (PEERS, SHARE, HD))
    out_ref[:, :, GROUP * HD : (GROUP + 1) * HD] = anchor
    out_ref[:, :, (GROUP + 1) * HD :] = anchor


def merge_parts(parts):
    return pl.pallas_call(
        merge_kernel,
        out_shape=pltpu.VMEM((PEERS, SHARE, SECOND), BF16),
        in_specs=[IN_VMEM],
        out_specs=IN_VMEM,
        name="merge_parts",
    )(vmem(parts))


def project_kernel(rows_ref, own_ref, mate_ref, out_ref, half_ref):
    core, unused = position_of()
    rows = rows_ref[:, :, : GROUP * HD].astype(F32).reshape(8, 2, 16, GROUP * HD)
    upper = rows[:, 0].reshape(128, GROUP * HD).astype(BF16)
    lower = rows[:, 1].reshape(128, GROUP * HD).astype(BF16)

    def packed(ref):
        pieces = [ref[WEIGHT + h * 64 : WEIGHT + (h + 1) * 64, :] for h in range(GROUP)]
        weight = jnp.concatenate(pieces, 1)
        zero = jnp.zeros_like(weight)
        left = jnp.concatenate([weight, zero], 0)
        right = jnp.concatenate([zero, weight], 0)
        return (nt(upper, left) + nt(lower, right)).reshape(8, 16, 128)

    out_ref[pl.ds(core, 1)] = packed(own_ref)[None]
    out_ref[pl.ds(1 - core, 1)] = packed(mate_ref)[None]
    half = rows_ref[:, :, GROUP * HD : (GROUP + 1) * HD].astype(F32)
    half_ref[...] = half.reshape(BLK, HD).astype(BF16)


def project(rows, own, mate):
    return pl.pallas_call(
        project_kernel,
        out_shape=(pltpu.VMEM((2, 8, 16, 128), F32), pltpu.VMEM((BLK, HD), BF16)),
        in_specs=[IN_VMEM] * 3,
        out_specs=(IN_VMEM, IN_VMEM),
        name="project",
    )(vmem(rows), vmem(own), vmem(mate))


def context_kernel(q_ref, own_ref, half_ref, other_ref, out_ref):
    core, block = position_of()
    has_anchor = block > 0
    half, other = half_ref[...].astype(F32), other_ref[...].astype(F32)
    anchor_keys = jnp.where(core == 0, half, other).astype(BF16)
    anchor_values = jnp.where(core == 0, other, half).astype(BF16)
    keys, values = own_ref[0:BLK, :], own_ref[BLK : 2 * BLK, :]
    row = lax.broadcasted_iota(jnp.int32, (BLK, BLK), 0)
    column = lax.broadcasted_iota(jnp.int32, (BLK, BLK), 1)
    for h in range(GROUP):
        q = q_ref[:, h * HD : (h + 1) * HD]
        own = jnp.where(row >= column, nt(q, keys) * SCALE, -jnp.inf)
        first = jnp.where(has_anchor, nt(q, anchor_keys) * SCALE, -jnp.inf)
        top = jnp.max(jnp.maximum(own, first), axis=-1, keepdims=True)
        own, first = jnp.exp(own - top), jnp.exp(first - top)
        total = jnp.sum(own + first, axis=-1, keepdims=True)
        summed = nn(own.astype(BF16), values) + nn(first.astype(BF16), anchor_values)
        out_ref[:, h * HD : (h + 1) * HD] = (summed / total).astype(BF16)


def context(queries, own, half, other):
    return pl.pallas_call(
        context_kernel,
        out_shape=jax.ShapeDtypeStruct((BLK, GROUP * HD), BF16),
        in_specs=[IN_VMEM] * 4,
        cost_estimate=pl.CostEstimate(
            flops=4 * BLK * GROUP * 2 * BLK * HD,
            transcendentals=BLK * GROUP * 2 * BLK,
            bytes_accessed=1 << 20,
        ),
        name="context",
    )(vmem(queries), vmem(own), vmem(half), vmem(other))


def finish_kernel(parts_ref, out_ref):
    for k in range(2):
        summed = jnp.sum(parts_ref[k * 8 : (k + 1) * 8], axis=0)
        out_ref[k * 32 : k * 32 + 16, :] = summed[:, :64].astype(BF16)
        out_ref[k * 32 + 16 : k * 32 + 32, :] = summed[:, 64:].astype(BF16)


def finish(parts):
    return pl.pallas_call(
        finish_kernel,
        out_shape=jax.ShapeDtypeStruct((64, 64), BF16),
        in_specs=[IN_VMEM],
        name="finish",
    )(vmem(parts))


def body(ctx_queries, ctx_keys, ctx_values, query_queries, query_keys, query_values, out_weight):
    own, rows = pack(ctx_keys, ctx_values, query_keys, query_values, out_weight.T, query_queries)
    mate = lax.ppermute(own, "core", [(0, 1), (1, 0)])

    summed, stats = query_own(rows, own)
    parts = query_parts(rows, own, mate, summed, stats)
    parts = lax.all_to_all(parts.reshape(PEERS, SHARE, FIRST), ("z", "x"), 0, 0)
    message = merge_parts(parts)
    gathered = lax.all_to_all(message, ("z", "x"), 0, 0)

    sums, half = project(gathered, own, mate)
    sums = lax.all_to_all(sums.reshape(16, 16, 128), ("core", "tp"), 0, 0)
    other = lax.ppermute(half, "core", [(0, 1), (1, 0)])
    ctx_out = context(ctx_queries, own, half, other)
    query_out = finish(sums)
    return (ctx_out, query_out)


def solution(mesh):
    fine = Mesh(mesh.devices.reshape(8, 4, 2, 8), ("z", "x", "core", "tp"))
    ctx = ("z", "x", "core")
    return jax.shard_map(
        body,
        mesh=fine,
        in_specs=(
            P(ctx, "tp"),
            P(ctx, "tp"),
            P(ctx, "tp"),
            P(None, "tp"),
            P(ctx, "tp"),
            P(ctx, "tp"),
            P("tp", ctx),
        ),
        out_specs=(P(ctx, "tp"), P("tp", ctx)),
        check_vma=False,
    )
```

```python
import jax
import jax.numpy as jnp
from jax import lax
from jax.experimental import pallas as pl
from jax.experimental.pallas import tpu as pltpu
from jax.sharding import Mesh
from jax.sharding import PartitionSpec as P

HD = 128
GROUP = 4
BLK = 256
QL = 512
SHARE = 8
PEERS = 32
HALF = QL // 2
SCALE = HD**-0.5
F32 = jnp.float32
BF16 = jnp.bfloat16

STATS = GROUP * HD
ANCHOR = STATS + HD
FIRST = ANCHOR + HD
SECOND = GROUP * HD + HD
TAIL = 2 * BLK
WEIGHT = TAIL + 2 * SHARE
PACKED = WEIGHT + GROUP * 64


def nt(a, b):
    return lax.dot_general(a, b, (((1,), (1,)), ((), ())), preferred_element_type=F32)


def nn(a, b):
    return lax.dot_general(a, b, (((1,), (0,)), ((), ())), preferred_element_type=F32)


def vmem(array):
    return pltpu.with_memory_space_constraint(array, pltpu.VMEM)


IN_VMEM = pl.BlockSpec(memory_space=pltpu.VMEM)


def position_of():
    core = lax.axis_index("core")
    return core, (lax.axis_index("z") * 4 + lax.axis_index("x")) * 2 + core


def pack_kernel(
    keys_ref, values_ref, query_keys_ref, query_values_ref, weight_ref, rows_ref, out_ref, half_ref
):
    out_ref[0:BLK, :] = keys_ref[...]
    out_ref[BLK : 2 * BLK, :] = values_ref[...]
    tail = jnp.concatenate([query_keys_ref[...].astype(F32), query_values_ref[...].astype(F32)], 0)
    out_ref[TAIL:WEIGHT, :] = tail.astype(BF16)
    for h in range(GROUP):
        start = WEIGHT + h * 64
        out_ref[start : start + 64, :] = weight_ref[:, h * HD : (h + 1) * HD]
    core, unused = position_of()
    half_ref[...] = rows_ref[:, pl.ds(core, 1)].reshape(HALF, GROUP * HD)


def pack(keys, values, query_keys, query_values, weight, rows):
    return pl.pallas_call(
        pack_kernel,
        out_shape=(pltpu.VMEM((PACKED, HD), BF16), pltpu.VMEM((HALF, GROUP * HD), BF16)),
        in_specs=[IN_VMEM] * 6,
        out_specs=(IN_VMEM, IN_VMEM),
        name="pack",
    )(keys, values, query_keys, query_values, weight, rows.reshape(8, 2, 32, GROUP * HD))


def query_kernel(rows_ref, own_ref, mate_ref, out_ref):
    core, block = position_of()
    mate = block + 1 - 2 * core
    rows = rows_ref[...]
    own_keys, own_values = own_ref[0:BLK, :], own_ref[BLK : 2 * BLK, :]
    mate_keys, mate_values = mate_ref[0:BLK, :], mate_ref[BLK : 2 * BLK, :]
    own_tail, mate_tail = own_ref[TAIL:WEIGHT, :].astype(F32), mate_ref[TAIL:WEIGHT, :].astype(F32)
    tail_keys = jnp.concatenate([own_tail[:SHARE], mate_tail[:SHARE]], 0).astype(BF16)
    tail_values = jnp.concatenate([own_tail[SHARE:], mate_tail[SHARE:]], 0).astype(BF16)

    index = lax.broadcasted_iota(jnp.int32, (HALF, 2 * SHARE), 0)
    position = (index // 32) * 64 + core * 32 + index % 32
    column = lax.broadcasted_iota(jnp.int32, (HALF, 2 * SHARE), 1)
    own_seen = (column < SHARE) & (position >= block * SHARE + column)
    mate_seen = (column >= SHARE) & (position >= mate * SHARE + column - SHARE)

    lane = lax.broadcasted_iota(jnp.int32, (HALF, HD), 1)
    stats = jnp.zeros((HALF, HD), F32)

    def attend(q, keys, values, tail, seen):
        scores = nt(q, keys) * SCALE
        tail = jnp.where(seen, tail, -jnp.inf)
        top = jnp.maximum(
            jnp.max(scores, axis=-1, keepdims=True), jnp.max(tail, axis=-1, keepdims=True)
        )
        weights, tail = jnp.exp(scores - top), jnp.exp(tail - top)
        total = jnp.sum(weights, axis=-1, keepdims=True) + jnp.sum(tail, axis=-1, keepdims=True)
        summed = nn(weights.astype(BF16), values) + nn(tail.astype(BF16), tail_values)
        return top, total, summed

    for h in range(GROUP):
        q = rows[:, h * HD : (h + 1) * HD]
        tail = nt(q, tail_keys) * SCALE
        top0, total0, summed0 = attend(q, own_keys, own_values, tail, own_seen)
        top1, total1, summed1 = attend(q, mate_keys, mate_values, tail, mate_seen)
        top = jnp.maximum(top0, top1)
        factor0, factor1 = jnp.exp(top0 - top), jnp.exp(top1 - top)
        out_ref[:, h * HD : (h + 1) * HD] = (summed0 * factor0 + summed1 * factor1).astype(BF16)
        total = total0 * factor0 + total1 * factor1
        first = top.astype(BF16).astype(F32)
        second = (top - first).astype(BF16).astype(F32)
        high = total.astype(BF16).astype(F32)
        terms = (first, second, top - first - second, high, total - high)
        for i, term in enumerate(terms):
            stats = jnp.where(lane == i * GROUP + h, term, stats)
    out_ref[:, STATS:ANCHOR] = stats.astype(BF16)

    @pl.when(core == 0)
    def _():
        out_ref[:, ANCHOR:FIRST] = own_keys

    @pl.when(core != 0)
    def _():
        out_ref[:, ANCHOR:FIRST] = mate_values


def query_parts(rows, own, mate):
    return pl.pallas_call(
        query_kernel,
        out_shape=pltpu.VMEM((HALF, FIRST), BF16),
        in_specs=[IN_VMEM] * 3,
        out_specs=IN_VMEM,
        name="query_parts",
    )(vmem(rows), vmem(own), vmem(mate))


def merge_kernel(parts_ref, out_ref):
    stats = parts_ref[:, :, STATS:ANCHOR].astype(F32)
    flat = stats.reshape(PEERS * SHARE, HD)
    top = flat + (pltpu.roll(flat, HD - GROUP, 1) + pltpu.roll(flat, HD - 2 * GROUP, 1))
    top = top.reshape(PEERS, SHARE, HD)
    factor = jnp.exp(top - jnp.max(top, axis=0, keepdims=True))
    for h in range(GROUP):
        weight = jnp.broadcast_to(factor[:, :, h : h + 1], (PEERS, SHARE, HD))
        totals = jnp.sum(weight * stats, axis=0)
        high, low = 3 * GROUP + h, 4 * GROUP + h
        total = totals[:, high : high + 1] + totals[:, low : low + 1]
        part = parts_ref[:, :, h * HD : (h + 1) * HD].astype(F32)
        attended = (jnp.sum(weight * part, axis=0) / total).astype(BF16)
        out_ref[:, :, h * HD : (h + 1) * HD] = jnp.broadcast_to(attended[None], (PEERS, SHARE, HD))
    anchor = jnp.broadcast_to(parts_ref[0, :, ANCHOR:FIRST][None], (PEERS, SHARE, HD))
    out_ref[:, :, GROUP * HD : (GROUP + 1) * HD] = anchor


def merge_parts(parts):
    return pl.pallas_call(
        merge_kernel,
        out_shape=pltpu.VMEM((PEERS, SHARE, SECOND), BF16),
        in_specs=[IN_VMEM],
        out_specs=IN_VMEM,
        name="merge_parts",
    )(vmem(parts))


def project_kernel(rows_ref, own_ref, mate_ref, out_ref, half_ref):
    core, unused = position_of()
    rows = rows_ref[:, :, : GROUP * HD].astype(F32).reshape(8, 2, 16, GROUP * HD)
    upper = rows[:, 0].reshape(128, GROUP * HD).astype(BF16)
    lower = rows[:, 1].reshape(128, GROUP * HD).astype(BF16)

    def packed(ref):
        pieces = [ref[WEIGHT + h * 64 : WEIGHT + (h + 1) * 64, :] for h in range(GROUP)]
        weight = jnp.concatenate(pieces, 1)
        zero = jnp.zeros_like(weight)
        left = jnp.concatenate([weight, zero], 0)
        right = jnp.concatenate([zero, weight], 0)
        return (nt(upper, left) + nt(lower, right)).reshape(8, 16, 128)

    out_ref[pl.ds(core, 1)] = packed(own_ref)[None]
    out_ref[pl.ds(1 - core, 1)] = packed(mate_ref)[None]
    half = rows_ref[:, :, GROUP * HD : (GROUP + 1) * HD].astype(F32)
    half_ref[...] = half.reshape(BLK, HD).astype(BF16)


def project(rows, own, mate):
    return pl.pallas_call(
        project_kernel,
        out_shape=(pltpu.VMEM((2, 8, 16, 128), F32), pltpu.VMEM((BLK, HD), BF16)),
        in_specs=[IN_VMEM] * 3,
        out_specs=(IN_VMEM, IN_VMEM),
        name="project",
    )(vmem(rows), vmem(own), vmem(mate))


def context_kernel(q_ref, own_ref, half_ref, other_ref, out_ref):
    core, block = position_of()
    has_anchor = block > 0
    half, other = half_ref[...].astype(F32), other_ref[...].astype(F32)
    anchor_keys = jnp.where(core == 0, half, other).astype(BF16)
    anchor_values = jnp.where(core == 0, other, half).astype(BF16)
    keys, values = own_ref[0:BLK, :], own_ref[BLK : 2 * BLK, :]
    row = lax.broadcasted_iota(jnp.int32, (BLK, BLK), 0)
    column = lax.broadcasted_iota(jnp.int32, (BLK, BLK), 1)
    for h in range(GROUP):
        q = q_ref[:, h * HD : (h + 1) * HD]
        own = jnp.where(row >= column, nt(q, keys) * SCALE, -jnp.inf)
        first = jnp.where(has_anchor, nt(q, anchor_keys) * SCALE, -jnp.inf)
        top = jnp.max(jnp.maximum(own, first), axis=-1, keepdims=True)
        own, first = jnp.exp(own - top), jnp.exp(first - top)
        total = jnp.sum(own + first, axis=-1, keepdims=True)
        summed = nn(own.astype(BF16), values) + nn(first.astype(BF16), anchor_values)
        out_ref[:, h * HD : (h + 1) * HD] = (summed / total).astype(BF16)


def context(queries, own, half, other):
    return pl.pallas_call(
        context_kernel,
        out_shape=jax.ShapeDtypeStruct((BLK, GROUP * HD), BF16),
        in_specs=[IN_VMEM] * 4,
        cost_estimate=pl.CostEstimate(
            flops=4 * BLK * GROUP * 2 * BLK * HD,
            transcendentals=BLK * GROUP * 2 * BLK,
            bytes_accessed=1 << 20,
        ),
        name="context",
    )(vmem(queries), vmem(own), vmem(half), vmem(other))


def finish_kernel(parts_ref, out_ref):
    for k in range(2):
        summed = jnp.sum(parts_ref[k * 8 : (k + 1) * 8], axis=0)
        out_ref[k * 32 : k * 32 + 16, :] = summed[:, :64].astype(BF16)
        out_ref[k * 32 + 16 : k * 32 + 32, :] = summed[:, 64:].astype(BF16)


def finish(parts):
    return pl.pallas_call(
        finish_kernel,
        out_shape=jax.ShapeDtypeStruct((64, 64), BF16),
        in_specs=[IN_VMEM],
        name="finish",
    )(vmem(parts))


def body(ctx_queries, ctx_keys, ctx_values, query_queries, query_keys, query_values, out_weight):
    own, rows = pack(ctx_keys, ctx_values, query_keys, query_values, out_weight.T, query_queries)
    mate = lax.ppermute(own, "core", [(0, 1), (1, 0)])

    parts = query_parts(rows, own, mate)
    parts = lax.all_to_all(parts.reshape(PEERS, SHARE, FIRST), ("z", "x"), 0, 0)
    message = merge_parts(parts)
    gathered = lax.all_to_all(message, ("z", "x"), 0, 0)

    sums, half = project(gathered, own, mate)
    sums = lax.all_to_all(sums.reshape(16, 16, 128), ("core", "tp"), 0, 0)
    other = lax.ppermute(half, "core", [(0, 1), (1, 0)])
    ctx_out = context(ctx_queries, own, half, other)
    query_out = finish(sums)
    return (ctx_out, query_out)


def solution(mesh):
    fine = Mesh(mesh.devices.reshape(8, 4, 2, 8), ("z", "x", "core", "tp"))
    ctx = ("z", "x", "core")
    return jax.shard_map(
        body,
        mesh=fine,
        in_specs=(
            P(ctx, "tp"),
            P(ctx, "tp"),
            P(ctx, "tp"),
            P(None, "tp"),
            P(ctx, "tp"),
            P(ctx, "tp"),
            P("tp", ctx),
        ),
        out_specs=(P(ctx, "tp"), P("tp", ctx)),
        check_vma=False,
    )
```

```python
import jax
import jax.numpy as jnp
from jax import lax
from jax.experimental import pallas as pl
from jax.experimental.pallas import tpu as pltpu
from jax.sharding import Mesh
from jax.sharding import PartitionSpec as P

HD = 128
GROUP = 4
BLK = 256
QL = 512
SHARE = 8
PEERS = 32
HALF = QL // 2
SCALE = HD**-0.5
F32 = jnp.float32
BF16 = jnp.bfloat16

STATS = GROUP * HD
ANCHOR = STATS + HD
FIRST = ANCHOR + HD
SECOND = GROUP * HD + HD
TAIL = 2 * BLK
WEIGHT = TAIL + 2 * SHARE
PACKED = WEIGHT + GROUP * 64


def nt(a, b):
    return lax.dot_general(a, b, (((1,), (1,)), ((), ())), preferred_element_type=F32)


def nn(a, b):
    return lax.dot_general(a, b, (((1,), (0,)), ((), ())), preferred_element_type=F32)


def vmem(array):
    return pltpu.with_memory_space_constraint(array, pltpu.VMEM)


IN_VMEM = pl.BlockSpec(memory_space=pltpu.VMEM)


def position_of():
    core = lax.axis_index("core")
    return core, (lax.axis_index("z") * 4 + lax.axis_index("x")) * 2 + core


def pack_kernel(keys, values, query_keys, query_values, weight, rows, out_ref, half_ref, tail_ref, sems):
    core, unused = position_of()
    pieces = [
        (keys, out_ref.at[0:BLK]),
        (values, out_ref.at[BLK:TAIL]),
        (rows.at[:, core], half_ref),
        (query_keys, tail_ref.at[0]),
        (query_values, tail_ref.at[1]),
    ]
    for h in range(GROUP):
        start = WEIGHT + h * 64
        pieces.append((weight.at[:, h * HD : (h + 1) * HD], out_ref.at[start : start + 64]))
    copies = [pltpu.make_async_copy(a, b, sems.at[i]) for i, (a, b) in enumerate(pieces)]
    for copy in copies:
        copy.start()
    for copy in copies:
        copy.wait()
    tail = tail_ref[...].astype(F32).reshape(2 * SHARE, HD)
    out_ref[TAIL:WEIGHT, :] = tail.astype(BF16)


def pack(keys, values, query_keys, query_values, weight, rows):
    packed, half = pl.pallas_call(
        pack_kernel,
        out_shape=(pltpu.VMEM((PACKED, HD), BF16), pltpu.VMEM((8, 32, GROUP * HD), BF16)),
        in_specs=[pl.BlockSpec(memory_space=pl.ANY)] * 6,
        out_specs=(IN_VMEM, IN_VMEM),
        scratch_shapes=[pltpu.VMEM((2, SHARE, HD), BF16), pltpu.SemaphoreType.DMA((9,))],
        name="pack",
    )(keys, values, query_keys, query_values, weight, rows.reshape(8, 2, 32, GROUP * HD))
    return packed, half.reshape(HALF, GROUP * HD)


def query_kernel(rows_ref, own_ref, mate_ref, out_ref):
    core, block = position_of()
    mate = block + 1 - 2 * core
    rows = rows_ref[...]
    own_keys, own_values = own_ref[0:BLK, :], own_ref[BLK : 2 * BLK, :]
    mate_keys, mate_values = mate_ref[0:BLK, :], mate_ref[BLK : 2 * BLK, :]
    own_tail, mate_tail = own_ref[TAIL:WEIGHT, :].astype(F32), mate_ref[TAIL:WEIGHT, :].astype(F32)
    spare = jnp.zeros((HD - 2 * SHARE, HD), F32)
    tail_keys = jnp.concatenate([own_tail[:SHARE], mate_tail[:SHARE], spare], 0).astype(BF16)
    tail_values = jnp.concatenate([own_tail[SHARE:], mate_tail[SHARE:], spare], 0).astype(BF16)

    index = lax.broadcasted_iota(jnp.int32, (HALF, HD), 0)
    position = (index // 32) * 64 + core * 32 + index % 32
    lane = lax.broadcasted_iota(jnp.int32, (HALF, HD), 1)
    key_position = jnp.where(lane < SHARE, block * SHARE + lane, mate * SHARE + lane - SHARE)
    seen = (lane < 2 * SHARE) & (position >= key_position)
    stats = jnp.zeros((HALF, HD), F32)

    for h in range(GROUP):
        q = rows[:, h * HD : (h + 1) * HD]
        own, other = nt(q, own_keys) * SCALE, nt(q, mate_keys) * SCALE
        tail = jnp.where(seen, nt(q, tail_keys) * SCALE, -jnp.inf)
        top0 = jnp.maximum(jnp.maximum(own[:, :HD], own[:, HD:]), tail)
        top0 = jnp.max(top0, axis=-1, keepdims=True)
        top1 = jnp.max(other, axis=-1, keepdims=True)
        own, tail, other = jnp.exp(own - top0), jnp.exp(tail - top0), jnp.exp(other - top1)
        total0 = jnp.sum(own[:, :HD] + own[:, HD:] + tail, axis=-1, keepdims=True)
        total1 = jnp.sum(other, axis=-1, keepdims=True)
        summed0 = nn(own.astype(BF16), own_values) + nn(tail.astype(BF16), tail_values)
        summed1 = nn(other.astype(BF16), mate_values)
        top = jnp.maximum(top0, top1)
        factor0, factor1 = jnp.exp(top0 - top), jnp.exp(top1 - top)
        out_ref[:, h * HD : (h + 1) * HD] = (summed0 * factor0 + summed1 * factor1).astype(BF16)
        total = total0 * factor0 + total1 * factor1
        first = top.astype(BF16).astype(F32)
        second = (top - first).astype(BF16).astype(F32)
        high = total.astype(BF16).astype(F32)
        terms = (first, second, top - first - second, high, total - high)
        for i, term in enumerate(terms):
            stats = jnp.where(lane == i * GROUP + h, term, stats)
    out_ref[:, STATS:ANCHOR] = stats.astype(BF16)

    @pl.when(core == 0)
    def _():
        out_ref[:, ANCHOR:FIRST] = own_keys

    @pl.when(core != 0)
    def _():
        out_ref[:, ANCHOR:FIRST] = mate_values


def query_parts(rows, own, mate):
    return pl.pallas_call(
        query_kernel,
        out_shape=pltpu.VMEM((HALF, FIRST), BF16),
        in_specs=[IN_VMEM] * 3,
        out_specs=IN_VMEM,
        name="query_parts",
    )(vmem(rows), vmem(own), vmem(mate))


def merge_kernel(parts_ref, out_ref):
    stats = parts_ref[:, :, STATS:ANCHOR].astype(F32)
    flat = stats.reshape(PEERS * SHARE, HD)
    top = flat + (pltpu.roll(flat, HD - GROUP, 1) + pltpu.roll(flat, HD - 2 * GROUP, 1))
    top = top.reshape(PEERS, SHARE, HD)
    factor = jnp.exp(top - jnp.max(top, axis=0, keepdims=True))
    for h in range(GROUP):
        weight = jnp.broadcast_to(factor[:, :, h : h + 1], (PEERS, SHARE, HD))
        totals = jnp.sum(weight * stats, axis=0)
        high, low = 3 * GROUP + h, 4 * GROUP + h
        total = totals[:, high : high + 1] + totals[:, low : low + 1]
        part = parts_ref[:, :, h * HD : (h + 1) * HD].astype(F32)
        attended = (jnp.sum(weight * part, axis=0) / total).astype(BF16)
        out_ref[:, :, h * HD : (h + 1) * HD] = jnp.broadcast_to(attended[None], (PEERS, SHARE, HD))
    anchor = jnp.broadcast_to(parts_ref[0, :, ANCHOR:FIRST][None], (PEERS, SHARE, HD))
    out_ref[:, :, GROUP * HD : (GROUP + 1) * HD] = anchor


def merge_parts(parts):
    return pl.pallas_call(
        merge_kernel,
        out_shape=pltpu.VMEM((PEERS, SHARE, SECOND), BF16),
        in_specs=[IN_VMEM],
        out_specs=IN_VMEM,
        name="merge_parts",
    )(vmem(parts))


def project_kernel(rows_ref, own_ref, mate_ref, out_ref, half_ref):
    core, unused = position_of()
    rows = rows_ref[:, :, : GROUP * HD].astype(F32).reshape(8, 2, 16, GROUP * HD)
    upper = rows[:, 0].reshape(128, GROUP * HD).astype(BF16)
    lower = rows[:, 1].reshape(128, GROUP * HD).astype(BF16)

    def packed(ref):
        pieces = [ref[WEIGHT + h * 64 : WEIGHT + (h + 1) * 64, :] for h in range(GROUP)]
        weight = jnp.concatenate(pieces, 1)
        zero = jnp.zeros_like(weight)
        left = jnp.concatenate([weight, zero], 0)
        right = jnp.concatenate([zero, weight], 0)
        return (nt(upper, left) + nt(lower, right)).reshape(8, 16, 128)

    out_ref[pl.ds(core, 1)] = packed(own_ref)[None]
    out_ref[pl.ds(1 - core, 1)] = packed(mate_ref)[None]
    half = rows_ref[:, :, GROUP * HD : (GROUP + 1) * HD].astype(F32)
    half_ref[...] = half.reshape(BLK, HD).astype(BF16)


def project(rows, own, mate):
    return pl.pallas_call(
        project_kernel,
        out_shape=(pltpu.VMEM((2, 8, 16, 128), F32), pltpu.VMEM((BLK, HD), BF16)),
        in_specs=[IN_VMEM] * 3,
        out_specs=(IN_VMEM, IN_VMEM),
        name="project",
    )(vmem(rows), vmem(own), vmem(mate))


def context_kernel(q_ref, own_ref, half_ref, other_ref, out_ref):
    core, block = position_of()
    has_anchor = block > 0
    half, other = half_ref[...].astype(F32), other_ref[...].astype(F32)
    anchor_keys = jnp.where(core == 0, half, other).astype(BF16)
    anchor_values = jnp.where(core == 0, other, half).astype(BF16)
    keys, values = own_ref[0:BLK, :], own_ref[BLK : 2 * BLK, :]
    row = lax.broadcasted_iota(jnp.int32, (BLK, BLK), 0)
    column = lax.broadcasted_iota(jnp.int32, (BLK, BLK), 1)
    for h in range(GROUP):
        q = q_ref[:, h * HD : (h + 1) * HD]
        own = jnp.where(row >= column, nt(q, keys) * SCALE, -jnp.inf)
        first = jnp.where(has_anchor, nt(q, anchor_keys) * SCALE, -jnp.inf)
        top = jnp.max(jnp.maximum(own, first), axis=-1, keepdims=True)
        own, first = jnp.exp(own - top), jnp.exp(first - top)
        total = jnp.sum(own + first, axis=-1, keepdims=True)
        summed = nn(own.astype(BF16), values) + nn(first.astype(BF16), anchor_values)
        out_ref[:, h * HD : (h + 1) * HD] = (summed / total).astype(BF16)


def context(queries, own, half, other):
    return pl.pallas_call(
        context_kernel,
        out_shape=jax.ShapeDtypeStruct((BLK, GROUP * HD), BF16),
        in_specs=[IN_VMEM] * 4,
        cost_estimate=pl.CostEstimate(
            flops=4 * BLK * GROUP * 2 * BLK * HD,
            transcendentals=BLK * GROUP * 2 * BLK,
            bytes_accessed=1 << 20,
        ),
        name="context",
    )(vmem(queries), vmem(own), vmem(half), vmem(other))


def finish_kernel(parts_ref, out_ref):
    for k in range(2):
        summed = jnp.sum(parts_ref[k * 8 : (k + 1) * 8], axis=0)
        out_ref[k * 32 : k * 32 + 16, :] = summed[:, :64].astype(BF16)
        out_ref[k * 32 + 16 : k * 32 + 32, :] = summed[:, 64:].astype(BF16)


def finish(parts):
    return pl.pallas_call(
        finish_kernel,
        out_shape=jax.ShapeDtypeStruct((64, 64), BF16),
        in_specs=[IN_VMEM],
        name="finish",
    )(vmem(parts))


def body(ctx_queries, ctx_keys, ctx_values, query_queries, query_keys, query_values, out_weight):
    own, rows = pack(ctx_keys, ctx_values, query_keys, query_values, out_weight.T, query_queries)
    mate = lax.ppermute(own, "core", [(0, 1), (1, 0)])

    parts = query_parts(rows, own, mate)
    parts = lax.all_to_all(parts.reshape(PEERS, SHARE, FIRST), ("z", "x"), 0, 0)
    message = merge_parts(parts)
    gathered = lax.all_to_all(message, ("z", "x"), 0, 0)

    sums, half = project(gathered, own, mate)
    sums = lax.all_to_all(sums.reshape(16, 16, 128), ("core", "tp"), 0, 0)
    other = lax.ppermute(half, "core", [(0, 1), (1, 0)])
    ctx_out = context(ctx_queries, own, half, other)
    query_out = finish(sums)
    return (ctx_out, query_out)


def solution(mesh):
    fine = Mesh(mesh.devices.reshape(8, 4, 2, 8), ("z", "x", "core", "tp"))
    ctx = ("z", "x", "core")
    return jax.shard_map(
        body,
        mesh=fine,
        in_specs=(
            P(ctx, "tp"),
            P(ctx, "tp"),
            P(ctx, "tp"),
            P(None, "tp"),
            P(ctx, "tp"),
            P(ctx, "tp"),
            P("tp", ctx),
        ),
        out_specs=(P(ctx, "tp"), P("tp", ctx)),
        check_vma=False,
    )
```

```python
import jax
import jax.numpy as jnp
from jax import lax
from jax.experimental import pallas as pl
from jax.experimental.pallas import tpu as pltpu
from jax.sharding import Mesh
from jax.sharding import PartitionSpec as P

HD = 128
GROUP = 4
BLK = 256
QL = 512
SHARE = 8
PEERS = 32
HALF = QL // 2
SCALE = HD**-0.5
F32 = jnp.float32
BF16 = jnp.bfloat16

STATS = GROUP * HD
ANCHOR = STATS + HD
FIRST = ANCHOR + HD
SECOND = GROUP * HD + HD
TAIL = 2 * BLK
WEIGHT = TAIL + 2 * SHARE
PACKED = WEIGHT + GROUP * 64


def nt(a, b):
    return lax.dot_general(a, b, (((1,), (1,)), ((), ())), preferred_element_type=F32)


def nn(a, b):
    return lax.dot_general(a, b, (((1,), (0,)), ((), ())), preferred_element_type=F32)


def vmem(array):
    return pltpu.with_memory_space_constraint(array, pltpu.VMEM)


IN_VMEM = pl.BlockSpec(memory_space=pltpu.VMEM)


def position_of():
    core = lax.axis_index("core")
    return core, (lax.axis_index("z") * 4 + lax.axis_index("x")) * 2 + core


def pack_kernel(keys, values, query_keys, query_values, weight, rows, out_ref, half_ref, tail_ref, sems):
    core, unused = position_of()
    pieces = [
        (keys, out_ref.at[0:BLK]),
        (values, out_ref.at[BLK:TAIL]),
        (rows.at[:, core], half_ref),
        (query_keys, tail_ref.at[0]),
        (query_values, tail_ref.at[1]),
    ]
    for h in range(GROUP):
        start = WEIGHT + h * 64
        pieces.append((weight.at[:, h * HD : (h + 1) * HD], out_ref.at[start : start + 64]))
    copies = [pltpu.make_async_copy(a, b, sems.at[i]) for i, (a, b) in enumerate(pieces)]
    for copy in copies:
        copy.start()
    for copy in copies:
        copy.wait()
    tail = tail_ref[...].astype(F32).reshape(2 * SHARE, HD)
    out_ref[TAIL:WEIGHT, :] = tail.astype(BF16)


def pack(keys, values, query_keys, query_values, weight, rows):
    packed, half = pl.pallas_call(
        pack_kernel,
        out_shape=(pltpu.VMEM((PACKED, HD), BF16), pltpu.VMEM((8, 32, GROUP * HD), BF16)),
        in_specs=[pl.BlockSpec(memory_space=pl.ANY)] * 6,
        out_specs=(IN_VMEM, IN_VMEM),
        scratch_shapes=[pltpu.VMEM((2, SHARE, HD), BF16), pltpu.SemaphoreType.DMA((9,))],
        name="pack",
    )(keys, values, query_keys, query_values, weight, rows.reshape(8, 2, 32, GROUP * HD))
    return packed, half.reshape(HALF, GROUP * HD)


def query_kernel(rows_ref, own_ref, mate_ref, out_ref):
    core, block = position_of()
    mate = block + 1 - 2 * core
    rows = rows_ref[...]
    own_keys, own_values = own_ref[0:BLK, :], own_ref[BLK : 2 * BLK, :]
    mate_keys, mate_values = mate_ref[0:BLK, :], mate_ref[BLK : 2 * BLK, :]
    own_tail, mate_tail = own_ref[TAIL:WEIGHT, :].astype(F32), mate_ref[TAIL:WEIGHT, :].astype(F32)
    spare = jnp.zeros((HD - 2 * SHARE, HD), F32)
    tail_keys = jnp.concatenate([own_tail[:SHARE], mate_tail[:SHARE], spare], 0).astype(BF16)
    tail_values = jnp.concatenate([own_tail[SHARE:], mate_tail[SHARE:], spare], 0).astype(BF16)

    index = lax.broadcasted_iota(jnp.int32, (HALF, HD), 0)
    position = (index // 32) * 64 + core * 32 + index % 32
    lane = lax.broadcasted_iota(jnp.int32, (HALF, HD), 1)
    key_position = jnp.where(lane < SHARE, block * SHARE + lane, mate * SHARE + lane - SHARE)
    seen = (lane < 2 * SHARE) & (position >= key_position)
    stats = jnp.zeros((HALF, HD), F32)

    q = jnp.concatenate([rows[:, h * HD : (h + 1) * HD] for h in range(GROUP)], 0)
    seen = jnp.concatenate([jnp.where(seen, 0.0, -jnp.inf)] * GROUP, 0)
    own, other = nt(q, own_keys) * SCALE, nt(q, mate_keys) * SCALE
    tail = nt(q, tail_keys) * SCALE + seen
    tops0 = jnp.maximum(jnp.maximum(own[:, :HD], own[:, HD:]), tail)
    tops0 = jnp.max(tops0, axis=-1, keepdims=True)
    tops1 = jnp.max(other, axis=-1, keepdims=True)
    own, tail, other = jnp.exp(own - tops0), jnp.exp(tail - tops0), jnp.exp(other - tops1)
    totals0 = jnp.sum(own[:, :HD] + own[:, HD:] + tail, axis=-1, keepdims=True)
    totals1 = jnp.sum(other, axis=-1, keepdims=True)
    summed0 = nn(own.astype(BF16), own_values) + nn(tail.astype(BF16), tail_values)
    summed1 = nn(other.astype(BF16), mate_values)
    tops = jnp.maximum(tops0, tops1)
    factor0, factor1 = jnp.exp(tops0 - tops), jnp.exp(tops1 - tops)
    summed = (summed0 * factor0 + summed1 * factor1).astype(BF16)
    totals = totals0 * factor0 + totals1 * factor1
    for h in range(GROUP):
        mine = slice(h * HALF, (h + 1) * HALF)
        out_ref[:, h * HD : (h + 1) * HD] = summed[mine]
        top, total = tops[mine], totals[mine]
        first = top.astype(BF16).astype(F32)
        second = (top - first).astype(BF16).astype(F32)
        high = total.astype(BF16).astype(F32)
        terms = (first, second, top - first - second, high, total - high)
        for i, term in enumerate(terms):
            stats = jnp.where(lane == i * GROUP + h, term, stats)
    out_ref[:, STATS:ANCHOR] = stats.astype(BF16)

    @pl.when(core == 0)
    def _():
        out_ref[:, ANCHOR:FIRST] = own_keys
        pl.delay(2000)

    @pl.when(core != 0)
    def _():
        out_ref[:, ANCHOR:FIRST] = mate_values


def query_parts(rows, own, mate):
    return pl.pallas_call(
        query_kernel,
        out_shape=pltpu.VMEM((HALF, FIRST), BF16),
        in_specs=[IN_VMEM] * 3,
        out_specs=IN_VMEM,
        name="query_parts",
    )(vmem(rows), vmem(own), vmem(mate))


def merge_kernel(parts_ref, out_ref):
    stats = parts_ref[:, :, STATS:ANCHOR].astype(F32)
    flat = stats.reshape(PEERS * SHARE, HD)
    top = flat + (pltpu.roll(flat, HD - GROUP, 1) + pltpu.roll(flat, HD - 2 * GROUP, 1))
    top = top.reshape(PEERS, SHARE, HD)
    factor = jnp.exp(top - jnp.max(top, axis=0, keepdims=True))
    for h in range(GROUP):
        weight = jnp.broadcast_to(factor[:, :, h : h + 1], (PEERS, SHARE, HD))
        totals = jnp.sum(weight * stats, axis=0)
        high, low = 3 * GROUP + h, 4 * GROUP + h
        total = totals[:, high : high + 1] + totals[:, low : low + 1]
        part = parts_ref[:, :, h * HD : (h + 1) * HD].astype(F32)
        attended = (jnp.sum(weight * part, axis=0) / total).astype(BF16)
        out_ref[:, :, h * HD : (h + 1) * HD] = jnp.broadcast_to(attended[None], (PEERS, SHARE, HD))
    anchor = jnp.broadcast_to(parts_ref[0, :, ANCHOR:FIRST][None], (PEERS, SHARE, HD))
    out_ref[:, :, GROUP * HD : (GROUP + 1) * HD] = anchor


def merge_parts(parts):
    return pl.pallas_call(
        merge_kernel,
        out_shape=pltpu.VMEM((PEERS, SHARE, SECOND), BF16),
        in_specs=[IN_VMEM],
        out_specs=IN_VMEM,
        name="merge_parts",
    )(vmem(parts))


def project_kernel(rows_ref, own_ref, mate_ref, out_ref, half_ref):
    core, unused = position_of()
    rows = rows_ref[:, :, : GROUP * HD].astype(F32).reshape(8, 2, 16, GROUP * HD)
    upper = rows[:, 0].reshape(128, GROUP * HD).astype(BF16)
    lower = rows[:, 1].reshape(128, GROUP * HD).astype(BF16)

    def packed(ref):
        pieces = [ref[WEIGHT + h * 64 : WEIGHT + (h + 1) * 64, :] for h in range(GROUP)]
        weight = jnp.concatenate(pieces, 1)
        zero = jnp.zeros_like(weight)
        left = jnp.concatenate([weight, zero], 0)
        right = jnp.concatenate([zero, weight], 0)
        return (nt(upper, left) + nt(lower, right)).reshape(8, 16, 128)

    out_ref[pl.ds(core, 1)] = packed(own_ref)[None]
    out_ref[pl.ds(1 - core, 1)] = packed(mate_ref)[None]
    half = rows_ref[:, :, GROUP * HD : (GROUP + 1) * HD].astype(F32)
    half_ref[...] = half.reshape(BLK, HD).astype(BF16)


def project(rows, own, mate):
    return pl.pallas_call(
        project_kernel,
        out_shape=(pltpu.VMEM((2, 8, 16, 128), F32), pltpu.VMEM((BLK, HD), BF16)),
        in_specs=[IN_VMEM] * 3,
        out_specs=(IN_VMEM, IN_VMEM),
        name="project",
    )(vmem(rows), vmem(own), vmem(mate))


def context_kernel(q_ref, own_ref, half_ref, other_ref, out_ref):
    core, block = position_of()
    has_anchor = block > 0
    half, other = half_ref[...].astype(F32), other_ref[...].astype(F32)
    anchor_keys = jnp.where(core == 0, half, other).astype(BF16)
    anchor_values = jnp.where(core == 0, other, half).astype(BF16)
    keys, values = own_ref[0:BLK, :], own_ref[BLK : 2 * BLK, :]
    row = lax.broadcasted_iota(jnp.int32, (BLK, BLK), 0)
    column = lax.broadcasted_iota(jnp.int32, (BLK, BLK), 1)
    for h in range(GROUP):
        q = q_ref[:, h * HD : (h + 1) * HD]
        own = jnp.where(row >= column, nt(q, keys) * SCALE, -jnp.inf)
        first = jnp.where(has_anchor, nt(q, anchor_keys) * SCALE, -jnp.inf)
        top = jnp.max(jnp.maximum(own, first), axis=-1, keepdims=True)
        own, first = jnp.exp(own - top), jnp.exp(first - top)
        total = jnp.sum(own + first, axis=-1, keepdims=True)
        summed = nn(own.astype(BF16), values) + nn(first.astype(BF16), anchor_values)
        out_ref[:, h * HD : (h + 1) * HD] = (summed / total).astype(BF16)


def context(queries, own, half, other):
    return pl.pallas_call(
        context_kernel,
        out_shape=jax.ShapeDtypeStruct((BLK, GROUP * HD), BF16),
        in_specs=[IN_VMEM] * 4,
        cost_estimate=pl.CostEstimate(
            flops=4 * BLK * GROUP * 2 * BLK * HD,
            transcendentals=BLK * GROUP * 2 * BLK,
            bytes_accessed=1 << 20,
        ),
        name="context",
    )(vmem(queries), vmem(own), vmem(half), vmem(other))


def finish_kernel(parts_ref, out_ref):
    for k in range(2):
        summed = jnp.sum(parts_ref[k * 8 : (k + 1) * 8], axis=0)
        out_ref[k * 32 : k * 32 + 16, :] = summed[:, :64].astype(BF16)
        out_ref[k * 32 + 16 : k * 32 + 32, :] = summed[:, 64:].astype(BF16)


def finish(parts):
    return pl.pallas_call(
        finish_kernel,
        out_shape=jax.ShapeDtypeStruct((64, 64), BF16),
        in_specs=[IN_VMEM],
        name="finish",
    )(vmem(parts))


def body(ctx_queries, ctx_keys, ctx_values, query_queries, query_keys, query_values, out_weight):
    own, rows = pack(ctx_keys, ctx_values, query_keys, query_values, out_weight.T, query_queries)
    mate = lax.ppermute(own, "core", [(0, 1), (1, 0)])

    parts = query_parts(rows, own, mate)
    parts = lax.all_to_all(parts.reshape(PEERS, SHARE, FIRST), ("z", "x"), 0, 0)
    message = merge_parts(parts)
    gathered = lax.all_to_all(message, ("z", "x"), 0, 0)

    sums, half = project(gathered, own, mate)
    sums = lax.all_to_all(sums.reshape(16, 16, 128), ("core", "tp"), 0, 0)
    other = lax.ppermute(half, "core", [(0, 1), (1, 0)])
    ctx_out = context(ctx_queries, own, half, other)
    query_out = finish(sums)
    return (ctx_out, query_out)


def solution(mesh):
    fine = Mesh(mesh.devices.reshape(8, 4, 2, 8), ("z", "x", "core", "tp"))
    ctx = ("z", "x", "core")
    return jax.shard_map(
        body,
        mesh=fine,
        in_specs=(
            P(ctx, "tp"),
            P(ctx, "tp"),
            P(ctx, "tp"),
            P(None, "tp"),
            P(ctx, "tp"),
            P(ctx, "tp"),
            P("tp", ctx),
        ),
        out_specs=(P(ctx, "tp"), P("tp", ctx)),
        check_vma=False,
    )
```

```python
import jax
import jax.numpy as jnp
from jax import lax
from jax.experimental import pallas as pl
from jax.experimental.pallas import tpu as pltpu
from jax.sharding import Mesh
from jax.sharding import PartitionSpec as P

HD = 128
GROUP = 4
BLK = 256
QL = 512
SHARE = 8
PEERS = 32
HALF = QL // 2
SCALE = HD**-0.5
F32 = jnp.float32
BF16 = jnp.bfloat16

STATS = GROUP * HD
ANCHOR = STATS + HD
FIRST = ANCHOR + HD
SECOND = GROUP * HD + HD
TAIL = 2 * BLK
WEIGHT = TAIL + 2 * SHARE
PACKED = WEIGHT + GROUP * 64


def nt(a, b):
    return lax.dot_general(a, b, (((1,), (1,)), ((), ())), preferred_element_type=F32)


def nn(a, b):
    return lax.dot_general(a, b, (((1,), (0,)), ((), ())), preferred_element_type=F32)


def vmem(array):
    return pltpu.with_memory_space_constraint(array, pltpu.VMEM)


IN_VMEM = pl.BlockSpec(memory_space=pltpu.VMEM)


def position_of():
    core = lax.axis_index("core")
    return core, (lax.axis_index("z") * 4 + lax.axis_index("x")) * 2 + core


def pack_kernel(keys, values, query_keys, query_values, weight, rows, out_ref, half_ref, tail_ref, sems):
    core, unused = position_of()
    pieces = [
        (keys, out_ref.at[0:BLK]),
        (values, out_ref.at[BLK:TAIL]),
        (rows.at[:, core], half_ref),
        (query_keys, tail_ref.at[0]),
        (query_values, tail_ref.at[1]),
    ]
    for h in range(GROUP):
        start = WEIGHT + h * 64
        pieces.append((weight.at[:, h * HD : (h + 1) * HD], out_ref.at[start : start + 64]))
    copies = [pltpu.make_async_copy(a, b, sems.at[i]) for i, (a, b) in enumerate(pieces)]
    for copy in copies:
        copy.start()
    for copy in copies:
        copy.wait()
    tail = tail_ref[...].astype(F32).reshape(2 * SHARE, HD)
    out_ref[TAIL:WEIGHT, :] = tail.astype(BF16)


def pack(keys, values, query_keys, query_values, weight, rows):
    packed, half = pl.pallas_call(
        pack_kernel,
        out_shape=(pltpu.VMEM((PACKED, HD), BF16), pltpu.VMEM((8, 32, GROUP * HD), BF16)),
        in_specs=[pl.BlockSpec(memory_space=pl.ANY)] * 6,
        out_specs=(IN_VMEM, IN_VMEM),
        scratch_shapes=[pltpu.VMEM((2, SHARE, HD), BF16), pltpu.SemaphoreType.DMA((9,))],
        name="pack",
    )(keys, values, query_keys, query_values, weight, rows.reshape(8, 2, 32, GROUP * HD))
    return packed, half.reshape(HALF, GROUP * HD)


def stacked(rows_ref):
    return jnp.concatenate([rows_ref[:, h * HD : (h + 1) * HD] for h in range(GROUP)], 0)


def spread(column):
    return jnp.broadcast_to(column, (GROUP * HALF, HD))


def own_kernel(rows_ref, own_ref, top_ref, total_ref, summed_ref):
    keys, values = own_ref[0:BLK, :], own_ref[BLK:TAIL, :]
    scores = nt(stacked(rows_ref), keys) * SCALE
    top = jnp.max(scores, axis=-1, keepdims=True)
    weights = jnp.exp(scores - top)
    top_ref[...] = spread(top)
    total_ref[...] = spread(jnp.sum(weights, axis=-1, keepdims=True))
    summed_ref[...] = nn(weights.astype(BF16), values)


def query_own(rows, own):
    return pl.pallas_call(
        own_kernel,
        out_shape=(pltpu.VMEM((GROUP * HALF, HD), F32),) * 3,
        in_specs=[IN_VMEM] * 2,
        out_specs=(IN_VMEM,) * 3,
        name="query_own",
    )(vmem(rows), vmem(own))


def mate_kernel(rows_ref, own_ref, mate_ref, top_ref, total_ref, summed_ref, out_ref):
    core, block = position_of()
    mate = block + 1 - 2 * core
    keys, values = mate_ref[0:BLK, :], mate_ref[BLK:TAIL, :]
    own_tail, mate_tail = own_ref[TAIL:WEIGHT, :].astype(F32), mate_ref[TAIL:WEIGHT, :].astype(F32)
    spare = jnp.zeros((HD - 2 * SHARE, HD), F32)
    tail_keys = jnp.concatenate([own_tail[:SHARE], mate_tail[:SHARE], spare], 0).astype(BF16)
    tail_values = jnp.concatenate([own_tail[SHARE:], mate_tail[SHARE:], spare], 0).astype(BF16)

    index = lax.broadcasted_iota(jnp.int32, (HALF, HD), 0)
    position = (index // 32) * 64 + core * 32 + index % 32
    lane = lax.broadcasted_iota(jnp.int32, (HALF, HD), 1)
    key_position = jnp.where(lane < SHARE, block * SHARE + lane, mate * SHARE + lane - SHARE)
    seen = (lane < 2 * SHARE) & (position >= key_position)
    seen = jnp.concatenate([jnp.where(seen, 0.0, -jnp.inf)] * GROUP, 0)

    q = stacked(rows_ref)
    scores = nt(q, keys) * SCALE
    tail = nt(q, tail_keys) * SCALE + seen
    top1 = jnp.maximum(jnp.maximum(scores[:, :HD], scores[:, HD:]), tail)
    top1 = jnp.max(top1, axis=-1, keepdims=True)
    weights, tail = jnp.exp(scores - top1), jnp.exp(tail - top1)
    total1 = jnp.sum(weights[:, :HD] + weights[:, HD:] + tail, axis=-1, keepdims=True)
    summed1 = nn(weights.astype(BF16), values) + nn(tail.astype(BF16), tail_values)
    top0, top1 = top_ref[...], spread(top1)
    tops = jnp.maximum(top0, top1)
    factor0, factor1 = jnp.exp(top0 - tops), jnp.exp(top1 - tops)
    summed = (summed_ref[...] * factor0 + summed1 * factor1).astype(BF16)
    totals = total_ref[...] * factor0 + spread(total1) * factor1

    stats = jnp.zeros((HALF, HD), F32)
    for h in range(GROUP):
        mine = slice(h * HALF, (h + 1) * HALF)
        out_ref[:, h * HD : (h + 1) * HD] = summed[mine]
        top, total = tops[mine], totals[mine]
        first = top.astype(BF16).astype(F32)
        second = (top - first).astype(BF16).astype(F32)
        high = total.astype(BF16).astype(F32)
        terms = (first, second, top - first - second, high, total - high)
        for i, term in enumerate(terms):
            stats = jnp.where(lane == i * GROUP + h, term, stats)
    out_ref[:, STATS:ANCHOR] = stats.astype(BF16)

    @pl.when(core == 0)
    def _():
        out_ref[:, ANCHOR:FIRST] = own_ref[0:BLK, :]
        pl.delay(2500)

    @pl.when(core != 0)
    def _():
        out_ref[:, ANCHOR:FIRST] = values


def query_parts(rows, own, mate, parts):
    return pl.pallas_call(
        mate_kernel,
        out_shape=pltpu.VMEM((HALF, FIRST), BF16),
        in_specs=[IN_VMEM] * 6,
        out_specs=IN_VMEM,
        name="query_parts",
    )(vmem(rows), vmem(own), vmem(mate), *(vmem(part) for part in parts))


def merge_kernel(parts_ref, out_ref):
    stats = parts_ref[:, :, STATS:ANCHOR].astype(F32)
    flat = stats.reshape(PEERS * SHARE, HD)
    top = flat + (pltpu.roll(flat, HD - GROUP, 1) + pltpu.roll(flat, HD - 2 * GROUP, 1))
    top = top.reshape(PEERS, SHARE, HD)
    factor = jnp.exp(top - jnp.max(top, axis=0, keepdims=True))
    for h in range(GROUP):
        weight = jnp.broadcast_to(factor[:, :, h : h + 1], (PEERS, SHARE, HD))
        totals = jnp.sum(weight * stats, axis=0)
        high, low = 3 * GROUP + h, 4 * GROUP + h
        total = totals[:, high : high + 1] + totals[:, low : low + 1]
        part = parts_ref[:, :, h * HD : (h + 1) * HD].astype(F32)
        attended = (jnp.sum(weight * part, axis=0) / total).astype(BF16)
        out_ref[:, :, h * HD : (h + 1) * HD] = jnp.broadcast_to(attended[None], (PEERS, SHARE, HD))
    anchor = jnp.broadcast_to(parts_ref[0, :, ANCHOR:FIRST][None], (PEERS, SHARE, HD))
    out_ref[:, :, GROUP * HD : (GROUP + 1) * HD] = anchor


def merge_parts(parts):
    return pl.pallas_call(
        merge_kernel,
        out_shape=pltpu.VMEM((PEERS, SHARE, SECOND), BF16),
        in_specs=[IN_VMEM],
        out_specs=IN_VMEM,
        name="merge_parts",
    )(vmem(parts))


def project_kernel(rows_ref, own_ref, mate_ref, out_ref):
    core, unused = position_of()
    rows = rows_ref[:, :, : GROUP * HD].astype(F32).reshape(8, 2, 16, GROUP * HD)
    upper = rows[:, 0].reshape(128, GROUP * HD).astype(BF16)
    lower = rows[:, 1].reshape(128, GROUP * HD).astype(BF16)

    def packed(ref):
        pieces = [ref[WEIGHT + h * 64 : WEIGHT + (h + 1) * 64, :] for h in range(GROUP)]
        weight = jnp.concatenate(pieces, 1)
        zero = jnp.zeros_like(weight)
        left = jnp.concatenate([weight, zero], 0)
        right = jnp.concatenate([zero, weight], 0)
        return (nt(upper, left) + nt(lower, right)).reshape(8, 16, 128)

    out_ref[pl.ds(core, 1)] = packed(own_ref)[None]
    out_ref[pl.ds(1 - core, 1)] = packed(mate_ref)[None]


def project(rows, own, mate):
    return pl.pallas_call(
        project_kernel,
        out_shape=pltpu.VMEM((2, 8, 16, 128), F32),
        in_specs=[IN_VMEM] * 3,
        out_specs=IN_VMEM,
        name="project",
    )(vmem(rows), vmem(own), vmem(mate))


def half_kernel(rows_ref, half_ref):
    half = rows_ref[:, :, GROUP * HD : (GROUP + 1) * HD].astype(F32)
    half_ref[...] = half.reshape(BLK, HD).astype(BF16)


def anchor_half(rows):
    return pl.pallas_call(
        half_kernel,
        out_shape=pltpu.VMEM((BLK, HD), BF16),
        in_specs=[IN_VMEM],
        out_specs=IN_VMEM,
        name="anchor_half",
    )(vmem(rows))


def context_kernel(q_ref, own_ref, half_ref, other_ref, out_ref):
    core, block = position_of()
    has_anchor = block > 0
    half, other = half_ref[...].astype(F32), other_ref[...].astype(F32)
    anchor_keys = jnp.where(core == 0, half, other).astype(BF16)
    anchor_values = jnp.where(core == 0, other, half).astype(BF16)
    keys, values = own_ref[0:BLK, :], own_ref[BLK : 2 * BLK, :]
    row = lax.broadcasted_iota(jnp.int32, (BLK, BLK), 0)
    column = lax.broadcasted_iota(jnp.int32, (BLK, BLK), 1)
    for h in range(GROUP):
        q = q_ref[:, h * HD : (h + 1) * HD]
        own = jnp.where(row >= column, nt(q, keys) * SCALE, -jnp.inf)
        first = jnp.where(has_anchor, nt(q, anchor_keys) * SCALE, -jnp.inf)
        top = jnp.max(jnp.maximum(own, first), axis=-1, keepdims=True)
        own, first = jnp.exp(own - top), jnp.exp(first - top)
        total = jnp.sum(own + first, axis=-1, keepdims=True)
        summed = nn(own.astype(BF16), values) + nn(first.astype(BF16), anchor_values)
        out_ref[:, h * HD : (h + 1) * HD] = (summed / total).astype(BF16)


def context(queries, own, half, other):
    return pl.pallas_call(
        context_kernel,
        out_shape=jax.ShapeDtypeStruct((BLK, GROUP * HD), BF16),
        in_specs=[IN_VMEM] * 4,
        cost_estimate=pl.CostEstimate(
            flops=4 * BLK * GROUP * 2 * BLK * HD,
            transcendentals=BLK * GROUP * 2 * BLK,
            bytes_accessed=1 << 20,
        ),
        name="context",
    )(vmem(queries), vmem(own), vmem(half), vmem(other))


def finish_kernel(parts_ref, out_ref):
    for k in range(2):
        summed = jnp.sum(parts_ref[k * 8 : (k + 1) * 8], axis=0)
        out_ref[k * 32 : k * 32 + 16, :] = summed[:, :64].astype(BF16)
        out_ref[k * 32 + 16 : k * 32 + 32, :] = summed[:, 64:].astype(BF16)


def finish(parts):
    return pl.pallas_call(
        finish_kernel,
        out_shape=jax.ShapeDtypeStruct((64, 64), BF16),
        in_specs=[IN_VMEM],
        name="finish",
    )(vmem(parts))


def body(ctx_queries, ctx_keys, ctx_values, query_queries, query_keys, query_values, out_weight):
    own, rows = pack(ctx_keys, ctx_values, query_keys, query_values, out_weight.T, query_queries)
    mate = lax.ppermute(own, "core", [(0, 1), (1, 0)])

    parts = query_parts(rows, own, mate, query_own(rows, own))
    parts = lax.all_to_all(parts.reshape(PEERS, SHARE, FIRST), ("x", "z"), 0, 0)
    message = merge_parts(parts)
    gathered = lax.all_to_all(message, ("x", "z"), 0, 0)

    sums = project(gathered, own, mate)
    half = anchor_half(gathered)
    sums = lax.all_to_all(sums.reshape(16, 16, 128), ("core", "tp"), 0, 0)
    other = lax.ppermute(half, "core", [(0, 1), (1, 0)])
    ctx_out = context(ctx_queries, own, half, other)
    query_out = finish(sums)
    return (ctx_out, query_out)


def solution(mesh):
    fine = Mesh(mesh.devices.reshape(8, 4, 2, 8), ("z", "x", "core", "tp"))
    ctx = ("z", "x", "core")
    return jax.shard_map(
        body,
        mesh=fine,
        in_specs=(
            P(ctx, "tp"),
            P(ctx, "tp"),
            P(ctx, "tp"),
            P(None, "tp"),
            P(ctx, "tp"),
            P(ctx, "tp"),
            P("tp", ctx),
        ),
        out_specs=(P(ctx, "tp"), P("tp", ctx)),
        check_vma=False,
    )
```

```python
import jax
import jax.numpy as jnp
from jax import lax
from jax.experimental import pallas as pl
from jax.experimental.pallas import tpu as pltpu
from jax.sharding import Mesh
from jax.sharding import PartitionSpec as P

HD = 128
GROUP = 4
BLK = 256
QL = 512
SHARE = 8
PEERS = 32
HALF = QL // 2
SCALE = HD**-0.5
F32 = jnp.float32
BF16 = jnp.bfloat16

STATS = GROUP * HD
ANCHOR = STATS + HD
FIRST = ANCHOR + HD
SECOND = GROUP * HD + HD
TAIL = 2 * BLK
WEIGHT = TAIL + 2 * SHARE
PACKED = WEIGHT + GROUP * 64


def nt(a, b):
    return lax.dot_general(a, b, (((1,), (1,)), ((), ())), preferred_element_type=F32)


def nn(a, b):
    return lax.dot_general(a, b, (((1,), (0,)), ((), ())), preferred_element_type=F32)


def vmem(array):
    return pltpu.with_memory_space_constraint(array, pltpu.VMEM)


IN_VMEM = pl.BlockSpec(memory_space=pltpu.VMEM)


def position_of():
    core = lax.axis_index("core")
    return core, ((lax.axis_index("za") * 2 + lax.axis_index("zb")) * 4 + lax.axis_index("x")) * 2 + core


def pack_kernel(keys, values, query_keys, query_values, weight, rows, out_ref, half_ref, tail_ref, sems):
    core, unused = position_of()
    pieces = [
        (keys, out_ref.at[0:BLK]),
        (values, out_ref.at[BLK:TAIL]),
        (rows.at[:, core], half_ref),
        (query_keys, tail_ref.at[0]),
        (query_values, tail_ref.at[1]),
    ]
    for h in range(GROUP):
        start = WEIGHT + h * 64
        pieces.append((weight.at[:, h * HD : (h + 1) * HD], out_ref.at[start : start + 64]))
    copies = [pltpu.make_async_copy(a, b, sems.at[i]) for i, (a, b) in enumerate(pieces)]
    for copy in copies:
        copy.start()
    for copy in copies:
        copy.wait()
    tail = tail_ref[...].astype(F32).reshape(2 * SHARE, HD)
    out_ref[TAIL:WEIGHT, :] = tail.astype(BF16)


def pack(keys, values, query_keys, query_values, weight, rows):
    packed, half = pl.pallas_call(
        pack_kernel,
        out_shape=(pltpu.VMEM((PACKED, HD), BF16), pltpu.VMEM((8, 32, GROUP * HD), BF16)),
        in_specs=[pl.BlockSpec(memory_space=pl.ANY)] * 6,
        out_specs=(IN_VMEM, IN_VMEM),
        scratch_shapes=[pltpu.VMEM((2, SHARE, HD), BF16), pltpu.SemaphoreType.DMA((9,))],
        name="pack",
    )(keys, values, query_keys, query_values, weight, rows.reshape(8, 2, 32, GROUP * HD))
    return packed, half.reshape(HALF, GROUP * HD)


def stacked(rows_ref):
    return jnp.concatenate([rows_ref[:, h * HD : (h + 1) * HD] for h in range(GROUP)], 0)


def spread(column):
    return jnp.broadcast_to(column, (GROUP * HALF, HD))


def own_kernel(rows_ref, own_ref, top_ref, total_ref, summed_ref):
    keys, values = own_ref[0:BLK, :], own_ref[BLK:TAIL, :]
    scores = nt(stacked(rows_ref), keys) * SCALE
    top = jnp.max(scores, axis=-1, keepdims=True)
    weights = jnp.exp(scores - top)
    top_ref[...] = spread(top)
    total_ref[...] = spread(jnp.sum(weights, axis=-1, keepdims=True))
    summed_ref[...] = nn(weights.astype(BF16), values)


def query_own(rows, own):
    return pl.pallas_call(
        own_kernel,
        out_shape=(pltpu.VMEM((GROUP * HALF, HD), F32),) * 3,
        in_specs=[IN_VMEM] * 2,
        out_specs=(IN_VMEM,) * 3,
        name="query_own",
    )(vmem(rows), vmem(own))


def mate_kernel(rows_ref, own_ref, mate_ref, top_ref, total_ref, summed_ref, out_ref):
    core, block = position_of()
    mate = block + 1 - 2 * core
    keys, values = mate_ref[0:BLK, :], mate_ref[BLK:TAIL, :]
    own_tail, mate_tail = own_ref[TAIL:WEIGHT, :].astype(F32), mate_ref[TAIL:WEIGHT, :].astype(F32)
    spare = jnp.zeros((HD - 2 * SHARE, HD), F32)
    tail_keys = jnp.concatenate([own_tail[:SHARE], mate_tail[:SHARE], spare], 0).astype(BF16)
    tail_values = jnp.concatenate([own_tail[SHARE:], mate_tail[SHARE:], spare], 0).astype(BF16)

    index = lax.broadcasted_iota(jnp.int32, (HALF, HD), 0)
    position = (index // 32) * 64 + core * 32 + index % 32
    lane = lax.broadcasted_iota(jnp.int32, (HALF, HD), 1)
    key_position = jnp.where(lane < SHARE, block * SHARE + lane, mate * SHARE + lane - SHARE)
    seen = (lane < 2 * SHARE) & (position >= key_position)
    seen = jnp.concatenate([jnp.where(seen, 0.0, -jnp.inf)] * GROUP, 0)

    q = stacked(rows_ref)
    scores = nt(q, keys) * SCALE
    tail = nt(q, tail_keys) * SCALE + seen
    top1 = jnp.maximum(jnp.maximum(scores[:, :HD], scores[:, HD:]), tail)
    top1 = jnp.max(top1, axis=-1, keepdims=True)
    weights, tail = jnp.exp(scores - top1), jnp.exp(tail - top1)
    total1 = jnp.sum(weights[:, :HD] + weights[:, HD:] + tail, axis=-1, keepdims=True)
    summed1 = nn(weights.astype(BF16), values) + nn(tail.astype(BF16), tail_values)
    top0, top1 = top_ref[...], spread(top1)
    tops = jnp.maximum(top0, top1)
    factor0, factor1 = jnp.exp(top0 - tops), jnp.exp(top1 - tops)
    summed = (summed_ref[...] * factor0 + summed1 * factor1).astype(BF16)
    totals = total_ref[...] * factor0 + spread(total1) * factor1

    stats = jnp.zeros((HALF, HD), F32)
    for h in range(GROUP):
        mine = slice(h * HALF, (h + 1) * HALF)
        out_ref[:, h * HD : (h + 1) * HD] = summed[mine]
        top, total = tops[mine], totals[mine]
        first = top.astype(BF16).astype(F32)
        second = (top - first).astype(BF16).astype(F32)
        high = total.astype(BF16).astype(F32)
        terms = (first, second, top - first - second, high, total - high)
        for i, term in enumerate(terms):
            stats = jnp.where(lane == i * GROUP + h, term, stats)
    out_ref[:, STATS:ANCHOR] = stats.astype(BF16)

    @pl.when(core == 0)
    def _():
        out_ref[:, ANCHOR:FIRST] = own_ref[0:BLK, :]
        pl.delay(2500)

    @pl.when(core != 0)
    def _():
        out_ref[:, ANCHOR:FIRST] = values


def query_parts(rows, own, mate, parts):
    return pl.pallas_call(
        mate_kernel,
        out_shape=pltpu.VMEM((HALF, FIRST), BF16),
        in_specs=[IN_VMEM] * 6,
        out_specs=IN_VMEM,
        name="query_parts",
    )(vmem(rows), vmem(own), vmem(mate), *(vmem(part) for part in parts))


def merge_kernel(parts_ref, out_ref):
    stats = parts_ref[:, :, STATS:ANCHOR].astype(F32)
    flat = stats.reshape(PEERS * SHARE, HD)
    top = flat + (pltpu.roll(flat, HD - GROUP, 1) + pltpu.roll(flat, HD - 2 * GROUP, 1))
    top = top.reshape(PEERS, SHARE, HD)
    factor = jnp.exp(top - jnp.max(top, axis=0, keepdims=True))
    for h in range(GROUP):
        weight = jnp.broadcast_to(factor[:, :, h : h + 1], (PEERS, SHARE, HD))
        totals = jnp.sum(weight * stats, axis=0)
        high, low = 3 * GROUP + h, 4 * GROUP + h
        total = totals[:, high : high + 1] + totals[:, low : low + 1]
        part = parts_ref[:, :, h * HD : (h + 1) * HD].astype(F32)
        attended = (jnp.sum(weight * part, axis=0) / total).astype(BF16)
        out_ref[:, :, h * HD : (h + 1) * HD] = jnp.broadcast_to(attended[None], (PEERS, SHARE, HD))
    anchor = jnp.broadcast_to(parts_ref[0, :, ANCHOR:FIRST][None], (PEERS, SHARE, HD))
    out_ref[:, :, GROUP * HD : (GROUP + 1) * HD] = anchor


def merge_parts(parts):
    return pl.pallas_call(
        merge_kernel,
        out_shape=pltpu.VMEM((PEERS, SHARE, SECOND), BF16),
        in_specs=[IN_VMEM],
        out_specs=IN_VMEM,
        name="merge_parts",
    )(vmem(parts))


def project_kernel(rows_ref, own_ref, mate_ref, out_ref):
    core, unused = position_of()
    rows = rows_ref[:, : GROUP * HD].reshape(8, 2, 16, GROUP * HD)
    upper = rows[:, 0].reshape(128, GROUP * HD)
    lower = rows[:, 1].reshape(128, GROUP * HD)

    def packed(ref):
        pieces = [ref[WEIGHT + h * 64 : WEIGHT + (h + 1) * 64, :] for h in range(GROUP)]
        weight = jnp.concatenate(pieces, 1)
        zero = jnp.zeros_like(weight)
        left = jnp.concatenate([weight, zero], 0)
        right = jnp.concatenate([zero, weight], 0)
        return (nt(upper, left) + nt(lower, right)).reshape(8, 16, 128)

    out_ref[pl.ds(core, 1)] = packed(own_ref)[None]
    out_ref[pl.ds(1 - core, 1)] = packed(mate_ref)[None]


def project(rows, own, mate):
    return pl.pallas_call(
        project_kernel,
        out_shape=pltpu.VMEM((2, 8, 16, 128), F32),
        in_specs=[IN_VMEM] * 3,
        out_specs=IN_VMEM,
        name="project",
    )(vmem(rows), vmem(own), vmem(mate))


def half_kernel(rows_ref, half_ref):
    half_ref[...] = rows_ref[:, GROUP * HD :]


def anchor_half(rows):
    return pl.pallas_call(
        half_kernel,
        out_shape=pltpu.VMEM((BLK, HD), BF16),
        in_specs=[IN_VMEM],
        out_specs=IN_VMEM,
        name="anchor_half",
    )(vmem(rows))


def context_kernel(q_ref, own_ref, half_ref, other_ref, out_ref):
    core, block = position_of()
    has_anchor = block > 0
    half, other = half_ref[...].astype(F32), other_ref[...].astype(F32)
    anchor_keys = jnp.where(core == 0, half, other).astype(BF16)
    anchor_values = jnp.where(core == 0, other, half).astype(BF16)
    keys, values = own_ref[0:BLK, :], own_ref[BLK : 2 * BLK, :]
    row = lax.broadcasted_iota(jnp.int32, (BLK, BLK), 0)
    column = lax.broadcasted_iota(jnp.int32, (BLK, BLK), 1)
    for h in range(GROUP):
        q = q_ref[:, h * HD : (h + 1) * HD]
        own = jnp.where(row >= column, nt(q, keys) * SCALE, -jnp.inf)
        first = jnp.where(has_anchor, nt(q, anchor_keys) * SCALE, -jnp.inf)
        top = jnp.max(jnp.maximum(own, first), axis=-1, keepdims=True)
        own, first = jnp.exp(own - top), jnp.exp(first - top)
        total = jnp.sum(own + first, axis=-1, keepdims=True)
        summed = nn(own.astype(BF16), values) + nn(first.astype(BF16), anchor_values)
        out_ref[:, h * HD : (h + 1) * HD] = (summed / total).astype(BF16)


def context(queries, own, half, other):
    return pl.pallas_call(
        context_kernel,
        out_shape=jax.ShapeDtypeStruct((BLK, GROUP * HD), BF16),
        in_specs=[IN_VMEM] * 4,
        cost_estimate=pl.CostEstimate(
            flops=4 * BLK * GROUP * 2 * BLK * HD,
            transcendentals=BLK * GROUP * 2 * BLK,
            bytes_accessed=1 << 20,
        ),
        name="context",
    )(vmem(queries), vmem(own), vmem(half), vmem(other))


def finish_kernel(parts_ref, out_ref):
    for k in range(2):
        summed = jnp.sum(parts_ref[k * 8 : (k + 1) * 8], axis=0)
        out_ref[k * 32 : k * 32 + 16, :] = summed[:, :64].astype(BF16)
        out_ref[k * 32 + 16 : k * 32 + 32, :] = summed[:, 64:].astype(BF16)


def finish(parts):
    return pl.pallas_call(
        finish_kernel,
        out_shape=jax.ShapeDtypeStruct((64, 64), BF16),
        in_specs=[IN_VMEM],
        name="finish",
    )(vmem(parts))


def body(ctx_queries, ctx_keys, ctx_values, query_queries, query_keys, query_values, out_weight):
    own, rows = pack(ctx_keys, ctx_values, query_keys, query_values, out_weight.T, query_queries)
    mate = lax.ppermute(own, "core", [(0, 1), (1, 0)])

    parts = query_parts(rows, own, mate, query_own(rows, own))
    parts = lax.all_to_all(parts.reshape(PEERS, SHARE, FIRST), ("x", "zb", "za"), 0, 0)
    message = merge_parts(parts)
    gathered = lax.all_to_all(message, ("x", "zb", "za"), 0, 0)

    gathered = gathered.reshape(HALF, SECOND)
    sums = project(gathered, own, mate)
    half = anchor_half(gathered)
    sums = lax.all_to_all(sums.reshape(16, 16, 128), ("core", "tp"), 0, 0)
    other = lax.ppermute(half, "core", [(0, 1), (1, 0)])
    ctx_out = context(ctx_queries, own, half, other)
    query_out = finish(sums)
    return (ctx_out, query_out)


def solution(mesh):
    fine = Mesh(mesh.devices.reshape(4, 2, 4, 2, 8), ("za", "zb", "x", "core", "tp"))
    ctx = ("za", "zb", "x", "core")
    return jax.shard_map(
        body,
        mesh=fine,
        in_specs=(
            P(ctx, "tp"),
            P(ctx, "tp"),
            P(ctx, "tp"),
            P(None, "tp"),
            P(ctx, "tp"),
            P(ctx, "tp"),
            P("tp", ctx),
        ),
        out_specs=(P(ctx, "tp"), P("tp", ctx)),
        check_vma=False,
    )
```

```python
import jax
import jax.numpy as jnp
from jax import lax
from jax.experimental import pallas as pl
from jax.experimental.pallas import tpu as pltpu
from jax.sharding import Mesh
from jax.sharding import PartitionSpec as P

HD = 128
GROUP = 4
BLK = 256
QL = 512
SHARE = 8
PEERS = 32
HALF = QL // 2
SCALE = HD**-0.5
F32 = jnp.float32
BF16 = jnp.bfloat16

STATS = GROUP * HD
ANCHOR = STATS + HD
FIRST = ANCHOR + HD
SECOND = GROUP * HD + HD
TAIL = 2 * BLK
WEIGHT = TAIL + 2 * SHARE
PACKED = WEIGHT + GROUP * 64


def nt(a, b):
    return lax.dot_general(a, b, (((1,), (1,)), ((), ())), preferred_element_type=F32)


def nn(a, b):
    return lax.dot_general(a, b, (((1,), (0,)), ((), ())), preferred_element_type=F32)


def vmem(array):
    return pltpu.with_memory_space_constraint(array, pltpu.VMEM)


IN_VMEM = pl.BlockSpec(memory_space=pltpu.VMEM)


def position_of():
    core = lax.axis_index("core")
    return core, ((lax.axis_index("za") * 2 + lax.axis_index("zb")) * 4 + lax.axis_index("x")) * 2 + core


def pack_kernel(keys, values, query_keys, query_values, weight, rows, out_ref, half_ref, tail_ref, sems):
    core, unused = position_of()
    pieces = [
        (keys, out_ref.at[0:BLK]),
        (values, out_ref.at[BLK:TAIL]),
        (rows.at[:, core], half_ref),
        (query_keys, tail_ref.at[0]),
        (query_values, tail_ref.at[1]),
    ]
    for h in range(GROUP):
        start = WEIGHT + h * 64
        pieces.append((weight.at[:, h * HD : (h + 1) * HD], out_ref.at[start : start + 64]))
    copies = [pltpu.make_async_copy(a, b, sems.at[i]) for i, (a, b) in enumerate(pieces)]
    for copy in copies:
        copy.start()
    for copy in copies:
        copy.wait()
    tail = tail_ref[...].astype(F32).reshape(2 * SHARE, HD)
    out_ref[TAIL:WEIGHT, :] = tail.astype(BF16)


def pack(keys, values, query_keys, query_values, weight, rows):
    packed, half = pl.pallas_call(
        pack_kernel,
        out_shape=(pltpu.VMEM((PACKED, HD), BF16), pltpu.VMEM((8, 32, GROUP * HD), BF16)),
        in_specs=[pl.BlockSpec(memory_space=pl.ANY)] * 6,
        out_specs=(IN_VMEM, IN_VMEM),
        scratch_shapes=[pltpu.VMEM((2, SHARE, HD), BF16), pltpu.SemaphoreType.DMA((9,))],
        name="pack",
    )(keys, values, query_keys, query_values, weight, rows.reshape(8, 2, 32, GROUP * HD))
    return packed, half.reshape(HALF, GROUP * HD)


def stacked(rows_ref):
    return jnp.concatenate([rows_ref[:, h * HD : (h + 1) * HD] for h in range(GROUP)], 0)


def spread(column):
    return jnp.broadcast_to(column, (GROUP * HALF, HD))


def own_kernel(rows_ref, own_ref, top_ref, total_ref, summed_ref):
    keys, values = own_ref[0:BLK, :], own_ref[BLK:TAIL, :]
    scores = nt(stacked(rows_ref), keys) * SCALE
    top = jnp.max(scores, axis=-1, keepdims=True)
    weights = jnp.exp(scores - top)
    top_ref[...] = spread(top)
    total_ref[...] = spread(jnp.sum(weights, axis=-1, keepdims=True))
    summed_ref[...] = nn(weights.astype(BF16), values)


def query_own(rows, own):
    return pl.pallas_call(
        own_kernel,
        out_shape=(pltpu.VMEM((GROUP * HALF, HD), F32),) * 3,
        in_specs=[IN_VMEM] * 2,
        out_specs=(IN_VMEM,) * 3,
        name="query_own",
    )(vmem(rows), vmem(own))


def mate_kernel(rows_ref, own_ref, mate_ref, top_ref, total_ref, summed_ref, out_ref):
    core, block = position_of()
    mate = block + 1 - 2 * core
    keys, values = mate_ref[0:BLK, :], mate_ref[BLK:TAIL, :]
    own_tail, mate_tail = own_ref[TAIL:WEIGHT, :].astype(F32), mate_ref[TAIL:WEIGHT, :].astype(F32)
    spare = jnp.zeros((HD - 2 * SHARE, HD), F32)
    tail_keys = jnp.concatenate([own_tail[:SHARE], mate_tail[:SHARE], spare], 0).astype(BF16)
    tail_values = jnp.concatenate([own_tail[SHARE:], mate_tail[SHARE:], spare], 0).astype(BF16)

    index = lax.broadcasted_iota(jnp.int32, (HALF, HD), 0)
    position = (index // 32) * 64 + core * 32 + index % 32
    lane = lax.broadcasted_iota(jnp.int32, (HALF, HD), 1)
    key_position = jnp.where(lane < SHARE, block * SHARE + lane, mate * SHARE + lane - SHARE)
    seen = (lane < 2 * SHARE) & (position >= key_position)
    seen = jnp.concatenate([jnp.where(seen, 0.0, -jnp.inf)] * GROUP, 0)

    q = stacked(rows_ref)
    scores = nt(q, keys) * SCALE
    tail = nt(q, tail_keys) * SCALE + seen
    top1 = jnp.maximum(jnp.maximum(scores[:, :HD], scores[:, HD:]), tail)
    top1 = jnp.max(top1, axis=-1, keepdims=True)
    weights, tail = jnp.exp(scores - top1), jnp.exp(tail - top1)
    total1 = jnp.sum(weights[:, :HD] + weights[:, HD:] + tail, axis=-1, keepdims=True)
    summed1 = nn(weights.astype(BF16), values) + nn(tail.astype(BF16), tail_values)
    top0, top1 = top_ref[...], spread(top1)
    tops = jnp.maximum(top0, top1)
    factor0, factor1 = jnp.exp(top0 - tops), jnp.exp(top1 - tops)
    summed = (summed_ref[...] * factor0 + summed1 * factor1).astype(BF16)
    totals = total_ref[...] * factor0 + spread(total1) * factor1

    packed = jnp.zeros((HALF, HD), F32)
    for h in range(GROUP):
        mine = slice(h * HALF, (h + 1) * HALF)
        out_ref[:, h * HD : (h + 1) * HD] = summed[mine]
        value = jnp.where(lane < 3 * GROUP, tops[mine], totals[mine])
        packed = jnp.where(lane % GROUP == h, value, packed)
    first = packed.astype(BF16).astype(F32)
    rest = packed - first
    second = rest.astype(BF16).astype(F32)
    stats = jnp.where(lane < 3 * GROUP, rest - second, jnp.where(lane < 4 * GROUP, first, rest))
    stats = jnp.where(lane < GROUP, first, jnp.where(lane < 2 * GROUP, second, stats))
    out_ref[:, STATS:ANCHOR] = stats.astype(BF16)

    @pl.when(core == 0)
    def _():
        out_ref[:, ANCHOR:FIRST] = own_ref[0:BLK, :]
        pl.delay(2500)

    @pl.when(core != 0)
    def _():
        out_ref[:, ANCHOR:FIRST] = values


def query_parts(rows, own, mate, parts):
    return pl.pallas_call(
        mate_kernel,
        out_shape=pltpu.VMEM((HALF, FIRST), BF16),
        in_specs=[IN_VMEM] * 6,
        out_specs=IN_VMEM,
        name="query_parts",
    )(vmem(rows), vmem(own), vmem(mate), *(vmem(part) for part in parts))


def merge_kernel(parts_ref, out_ref):
    stats = parts_ref[:, :, STATS:ANCHOR].astype(F32)
    flat = stats.reshape(PEERS * SHARE, HD)
    top = flat + (pltpu.roll(flat, HD - GROUP, 1) + pltpu.roll(flat, HD - 2 * GROUP, 1))
    top = top.reshape(PEERS, SHARE, HD)
    factor = jnp.exp(top - jnp.max(top, axis=0, keepdims=True))
    for h in range(GROUP):
        weight = jnp.broadcast_to(factor[:, :, h : h + 1], (PEERS, SHARE, HD))
        totals = jnp.sum(weight * stats, axis=0)
        high, low = 3 * GROUP + h, 4 * GROUP + h
        total = totals[:, high : high + 1] + totals[:, low : low + 1]
        part = parts_ref[:, :, h * HD : (h + 1) * HD].astype(F32)
        attended = (jnp.sum(weight * part, axis=0) / total).astype(BF16)
        out_ref[:, :, h * HD : (h + 1) * HD] = jnp.broadcast_to(attended[None], (PEERS, SHARE, HD))
    anchor = jnp.broadcast_to(parts_ref[0, :, ANCHOR:FIRST][None], (PEERS, SHARE, HD))
    out_ref[:, :, GROUP * HD : (GROUP + 1) * HD] = anchor


def merge_parts(parts):
    return pl.pallas_call(
        merge_kernel,
        out_shape=pltpu.VMEM((PEERS, SHARE, SECOND), BF16),
        in_specs=[IN_VMEM],
        out_specs=IN_VMEM,
        name="merge_parts",
    )(vmem(parts))


def project_kernel(rows_ref, own_ref, mate_ref, out_ref):
    core, unused = position_of()
    rows = rows_ref[:, : GROUP * HD].reshape(8, 2, 16, GROUP * HD)
    upper = rows[:, 0].reshape(128, GROUP * HD)
    lower = rows[:, 1].reshape(128, GROUP * HD)

    def packed(ref):
        pieces = [ref[WEIGHT + h * 64 : WEIGHT + (h + 1) * 64, :] for h in range(GROUP)]
        weight = jnp.concatenate(pieces, 1)
        zero = jnp.zeros_like(weight)
        left = jnp.concatenate([weight, zero], 0)
        right = jnp.concatenate([zero, weight], 0)
        return (nt(upper, left) + nt(lower, right)).reshape(8, 16, 128)

    out_ref[pl.ds(core, 1)] = packed(own_ref)[None]
    out_ref[pl.ds(1 - core, 1)] = packed(mate_ref)[None]


def project(rows, own, mate):
    return pl.pallas_call(
        project_kernel,
        out_shape=pltpu.VMEM((2, 8, 16, 128), F32),
        in_specs=[IN_VMEM] * 3,
        out_specs=IN_VMEM,
        name="project",
    )(vmem(rows), vmem(own), vmem(mate))


def half_kernel(rows_ref, half_ref):
    half_ref[...] = rows_ref[:, GROUP * HD :]


def anchor_half(rows):
    return pl.pallas_call(
        half_kernel,
        out_shape=pltpu.VMEM((BLK, HD), BF16),
        in_specs=[IN_VMEM],
        out_specs=IN_VMEM,
        name="anchor_half",
    )(vmem(rows))


def context_kernel(q_ref, own_ref, half_ref, other_ref, out_ref):
    core, block = position_of()
    has_anchor = block > 0
    half, other = half_ref[...].astype(F32), other_ref[...].astype(F32)
    anchor_keys = jnp.where(core == 0, half, other).astype(BF16)
    anchor_values = jnp.where(core == 0, other, half).astype(BF16)
    keys, values = own_ref[0:BLK, :], own_ref[BLK : 2 * BLK, :]
    row = lax.broadcasted_iota(jnp.int32, (BLK, BLK), 0)
    column = lax.broadcasted_iota(jnp.int32, (BLK, BLK), 1)
    for h in range(GROUP):
        q = q_ref[:, h * HD : (h + 1) * HD]
        own = jnp.where(row >= column, nt(q, keys) * SCALE, -jnp.inf)
        first = jnp.where(has_anchor, nt(q, anchor_keys) * SCALE, -jnp.inf)
        top = jnp.max(jnp.maximum(own, first), axis=-1, keepdims=True)
        own, first = jnp.exp(own - top), jnp.exp(first - top)
        total = jnp.sum(own + first, axis=-1, keepdims=True)
        summed = nn(own.astype(BF16), values) + nn(first.astype(BF16), anchor_values)
        out_ref[:, h * HD : (h + 1) * HD] = (summed / total).astype(BF16)


def context(queries, own, half, other):
    return pl.pallas_call(
        context_kernel,
        out_shape=jax.ShapeDtypeStruct((BLK, GROUP * HD), BF16),
        in_specs=[IN_VMEM] * 4,
        cost_estimate=pl.CostEstimate(
            flops=4 * BLK * GROUP * 2 * BLK * HD,
            transcendentals=BLK * GROUP * 2 * BLK,
            bytes_accessed=1 << 20,
        ),
        name="context",
    )(vmem(queries), vmem(own), vmem(half), vmem(other))


def finish_kernel(parts_ref, out_ref):
    for k in range(2):
        summed = jnp.sum(parts_ref[k * 8 : (k + 1) * 8], axis=0)
        out_ref[k * 32 : k * 32 + 16, :] = summed[:, :64].astype(BF16)
        out_ref[k * 32 + 16 : k * 32 + 32, :] = summed[:, 64:].astype(BF16)


def finish(parts):
    return pl.pallas_call(
        finish_kernel,
        out_shape=jax.ShapeDtypeStruct((64, 64), BF16),
        in_specs=[IN_VMEM],
        name="finish",
    )(vmem(parts))


def body(ctx_queries, ctx_keys, ctx_values, query_queries, query_keys, query_values, out_weight):
    own, rows = pack(ctx_keys, ctx_values, query_keys, query_values, out_weight.T, query_queries)
    mate = lax.ppermute(own, "core", [(0, 1), (1, 0)])

    parts = query_parts(rows, own, mate, query_own(rows, own))
    parts = lax.all_to_all(parts.reshape(PEERS, SHARE, FIRST), ("x", "zb", "za"), 0, 0)
    message = merge_parts(parts)
    gathered = lax.all_to_all(message, ("x", "zb", "za"), 0, 0)

    gathered = gathered.reshape(HALF, SECOND)
    sums = project(gathered, own, mate)
    half = anchor_half(gathered)
    sums = lax.all_to_all(sums.reshape(16, 16, 128), ("core", "tp"), 0, 0)
    other = lax.ppermute(half, "core", [(0, 1), (1, 0)])
    ctx_out = context(ctx_queries, own, half, other)
    query_out = finish(sums)
    return (ctx_out, query_out)


def solution(mesh):
    fine = Mesh(mesh.devices.reshape(4, 2, 4, 2, 8), ("za", "zb", "x", "core", "tp"))
    ctx = ("za", "zb", "x", "core")
    return jax.shard_map(
        body,
        mesh=fine,
        in_specs=(
            P(ctx, "tp"),
            P(ctx, "tp"),
            P(ctx, "tp"),
            P(None, "tp"),
            P(ctx, "tp"),
            P(ctx, "tp"),
            P("tp", ctx),
        ),
        out_specs=(P(ctx, "tp"), P("tp", ctx)),
        check_vma=False,
    )
```

```python
import jax
import jax.numpy as jnp
from jax import lax
from jax.experimental import pallas as pl
from jax.experimental.pallas import tpu as pltpu
from jax.sharding import Mesh
from jax.sharding import PartitionSpec as P

HD = 128
GROUP = 4
BLK = 256
QL = 512
SHARE = 8
PEERS = 32
HALF = QL // 2
SCALE = HD**-0.5
F32 = jnp.float32
BF16 = jnp.bfloat16

STATS = GROUP * HD
ANCHOR = STATS + HD
FIRST = ANCHOR + HD
SECOND = GROUP * HD + HD
TAIL = 2 * BLK
WEIGHT = TAIL + 2 * SHARE
PACKED = WEIGHT + GROUP * 64


def nt(a, b):
    return lax.dot_general(a, b, (((1,), (1,)), ((), ())), preferred_element_type=F32)


def nn(a, b):
    return lax.dot_general(a, b, (((1,), (0,)), ((), ())), preferred_element_type=F32)


def vmem(array):
    return pltpu.with_memory_space_constraint(array, pltpu.VMEM)


IN_VMEM = pl.BlockSpec(memory_space=pltpu.VMEM)


def position_of():
    core = lax.axis_index("core")
    return core, ((lax.axis_index("za") * 2 + lax.axis_index("zb")) * 4 + lax.axis_index("x")) * 2 + core


def pack_kernel(keys, values, query_keys, query_values, weight, rows, out_ref, half_ref, tail_ref, sems):
    core, unused = position_of()
    pieces = [
        (keys, out_ref.at[0:BLK]),
        (values, out_ref.at[BLK:TAIL]),
        (rows.at[:, core], half_ref),
        (query_keys, tail_ref.at[0]),
        (query_values, tail_ref.at[1]),
    ]
    for h in range(GROUP):
        start = WEIGHT + h * 64
        pieces.append((weight.at[:, h * HD : (h + 1) * HD], out_ref.at[start : start + 64]))
    copies = [pltpu.make_async_copy(a, b, sems.at[i]) for i, (a, b) in enumerate(pieces)]
    for copy in copies:
        copy.start()
    for copy in copies:
        copy.wait()
    tail = tail_ref[...].astype(F32).reshape(2 * SHARE, HD)
    out_ref[TAIL:WEIGHT, :] = tail.astype(BF16)


def pack(keys, values, query_keys, query_values, weight, rows):
    packed, half = pl.pallas_call(
        pack_kernel,
        out_shape=(pltpu.VMEM((PACKED, HD), BF16), pltpu.VMEM((8, 32, GROUP * HD), BF16)),
        in_specs=[pl.BlockSpec(memory_space=pl.ANY)] * 6,
        out_specs=(IN_VMEM, IN_VMEM),
        scratch_shapes=[pltpu.VMEM((2, SHARE, HD), BF16), pltpu.SemaphoreType.DMA((9,))],
        name="pack",
    )(keys, values, query_keys, query_values, weight, rows.reshape(8, 2, 32, GROUP * HD))
    return packed, half.reshape(HALF, GROUP * HD)


def stacked(rows_ref):
    return jnp.concatenate([rows_ref[:, h * HD : (h + 1) * HD] for h in range(GROUP)], 0)


def spread(column):
    return jnp.broadcast_to(column, (GROUP * HALF, HD))


def own_kernel(rows_ref, own_ref, top_ref, total_ref, summed_ref):
    keys, values = own_ref[0:BLK, :], own_ref[BLK:TAIL, :]
    scores = nt(stacked(rows_ref), keys) * SCALE
    top = jnp.max(scores, axis=-1, keepdims=True)
    weights = jnp.exp(scores - top)
    top_ref[...] = spread(top)
    total_ref[...] = spread(jnp.sum(weights, axis=-1, keepdims=True))
    summed_ref[...] = nn(weights.astype(BF16), values)


def query_own(rows, own):
    return pl.pallas_call(
        own_kernel,
        out_shape=(pltpu.VMEM((GROUP * HALF, HD), F32),) * 3,
        in_specs=[IN_VMEM] * 2,
        out_specs=(IN_VMEM,) * 3,
        name="query_own",
    )(vmem(rows), vmem(own))


def mate_kernel(rows_ref, own_ref, mate_ref, top_ref, total_ref, summed_ref, out_ref):
    core, block = position_of()
    mate = block + 1 - 2 * core
    keys, values = mate_ref[0:BLK, :], mate_ref[BLK:TAIL, :]
    own_tail, mate_tail = own_ref[TAIL:WEIGHT, :].astype(F32), mate_ref[TAIL:WEIGHT, :].astype(F32)
    spare = jnp.zeros((HD - 2 * SHARE, HD), F32)
    tail_keys = jnp.concatenate([own_tail[:SHARE], mate_tail[:SHARE], spare], 0).astype(BF16)
    tail_values = jnp.concatenate([own_tail[SHARE:], mate_tail[SHARE:], spare], 0).astype(BF16)

    index = lax.broadcasted_iota(jnp.int32, (HALF, HD), 0)
    position = (index // 32) * 64 + core * 32 + index % 32
    lane = lax.broadcasted_iota(jnp.int32, (HALF, HD), 1)
    key_position = jnp.where(lane < SHARE, block * SHARE + lane, mate * SHARE + lane - SHARE)
    seen = (lane < 2 * SHARE) & (position >= key_position)
    seen = jnp.concatenate([jnp.where(seen, 0.0, -jnp.inf)] * GROUP, 0)

    q = stacked(rows_ref)
    scores = nt(q, keys) * SCALE
    tail = nt(q, tail_keys) * SCALE + seen
    top1 = jnp.maximum(jnp.maximum(scores[:, :HD], scores[:, HD:]), tail)
    top1 = jnp.max(top1, axis=-1, keepdims=True)
    weights, tail = jnp.exp(scores - top1), jnp.exp(tail - top1)
    total1 = jnp.sum(weights[:, :HD] + weights[:, HD:] + tail, axis=-1, keepdims=True)
    summed1 = nn(weights.astype(BF16), values) + nn(tail.astype(BF16), tail_values)
    top0, top1 = top_ref[...], spread(top1)
    tops = jnp.maximum(top0, top1)
    factor0, factor1 = jnp.exp(top0 - tops), jnp.exp(top1 - tops)
    summed = (summed_ref[...] * factor0 + summed1 * factor1).astype(BF16)
    totals = total_ref[...] * factor0 + spread(total1) * factor1

    stats = jnp.zeros((HALF, HD), F32)
    for h in range(GROUP):
        mine = slice(h * HALF, (h + 1) * HALF)
        out_ref[:, h * HD : (h + 1) * HD] = summed[mine]
        top, total = tops[mine], totals[mine]
        first = top.astype(BF16).astype(F32)
        second = (top - first).astype(BF16).astype(F32)
        high = total.astype(BF16).astype(F32)
        terms = (first, second, top - first - second, high, total - high)
        for i, term in enumerate(terms):
            stats = jnp.where(lane == i * GROUP + h, term, stats)
    out_ref[:, STATS:ANCHOR] = stats.astype(BF16)

    @pl.when(core == 0)
    def _():
        out_ref[:, ANCHOR:FIRST] = own_ref[0:BLK, :]
        pl.delay(2500)

    @pl.when(core != 0)
    def _():
        out_ref[:, ANCHOR:FIRST] = values


def query_parts(rows, own, mate, parts):
    return pl.pallas_call(
        mate_kernel,
        out_shape=pltpu.VMEM((HALF, FIRST), BF16),
        in_specs=[IN_VMEM] * 6,
        out_specs=IN_VMEM,
        name="query_parts",
    )(vmem(rows), vmem(own), vmem(mate), *(vmem(part) for part in parts))


def merge_kernel(parts_ref, out_ref):
    stats = parts_ref[:, :, STATS:ANCHOR].astype(F32)
    flat = stats.reshape(PEERS * SHARE, HD)
    top = flat + (pltpu.roll(flat, HD - GROUP, 1) + pltpu.roll(flat, HD - 2 * GROUP, 1))
    top = top.reshape(PEERS, SHARE, HD)
    factor = jnp.exp(top - jnp.max(top, axis=0, keepdims=True))
    for h in range(GROUP):
        weight = jnp.broadcast_to(factor[:, :, h : h + 1], (PEERS, SHARE, HD))
        totals = jnp.sum(weight * stats, axis=0)
        high, low = 3 * GROUP + h, 4 * GROUP + h
        total = totals[:, high : high + 1] + totals[:, low : low + 1]
        part = parts_ref[:, :, h * HD : (h + 1) * HD].astype(F32)
        attended = (jnp.sum(weight * part, axis=0) / total).astype(BF16)
        out_ref[:, :, h * HD : (h + 1) * HD] = jnp.broadcast_to(attended[None], (PEERS, SHARE, HD))
    anchor = jnp.broadcast_to(parts_ref[0, :, ANCHOR:FIRST][None], (PEERS, SHARE, HD))
    out_ref[:, :, GROUP * HD : (GROUP + 1) * HD] = anchor


def merge_parts(parts):
    return pl.pallas_call(
        merge_kernel,
        out_shape=pltpu.VMEM((PEERS, SHARE, SECOND), BF16),
        in_specs=[IN_VMEM],
        out_specs=IN_VMEM,
        name="merge_parts",
    )(vmem(parts))


def project_kernel(rows_ref, own_ref, mate_ref, out_ref):
    core, unused = position_of()
    rows = rows_ref[:, : GROUP * HD].reshape(8, 2, 16, GROUP * HD)
    upper = rows[:, 0].reshape(128, GROUP * HD)
    lower = rows[:, 1].reshape(128, GROUP * HD)

    def weight(ref):
        pieces = [ref[WEIGHT + h * 64 : WEIGHT + (h + 1) * 64, :] for h in range(GROUP)]
        return jnp.concatenate(pieces, 1)

    own, mate = weight(own_ref), weight(mate_ref)
    zero = jnp.zeros_like(own)
    sums = nt(upper, jnp.concatenate([own, zero, mate, zero], 0))
    sums = sums + nt(lower, jnp.concatenate([zero, own, zero, mate], 0))
    out_ref[pl.ds(core, 1)] = sums[:, :HD].reshape(1, 8, 16, 128)
    out_ref[pl.ds(1 - core, 1)] = sums[:, HD:].reshape(1, 8, 16, 128)


def project(rows, own, mate):
    return pl.pallas_call(
        project_kernel,
        out_shape=pltpu.VMEM((2, 8, 16, 128), F32),
        in_specs=[IN_VMEM] * 3,
        out_specs=IN_VMEM,
        name="project",
    )(vmem(rows), vmem(own), vmem(mate))


def half_kernel(rows_ref, half_ref):
    half_ref[...] = rows_ref[:, GROUP * HD :]


def anchor_half(rows):
    return pl.pallas_call(
        half_kernel,
        out_shape=pltpu.VMEM((BLK, HD), BF16),
        in_specs=[IN_VMEM],
        out_specs=IN_VMEM,
        name="anchor_half",
    )(vmem(rows))


def context_kernel(q_ref, own_ref, half_ref, other_ref, out_ref):
    core, block = position_of()
    has_anchor = block > 0
    half, other = half_ref[...].astype(F32), other_ref[...].astype(F32)
    anchor_keys = jnp.where(core == 0, half, other).astype(BF16)
    anchor_values = jnp.where(core == 0, other, half).astype(BF16)
    keys, values = own_ref[0:BLK, :], own_ref[BLK : 2 * BLK, :]
    row = lax.broadcasted_iota(jnp.int32, (BLK, BLK), 0)
    column = lax.broadcasted_iota(jnp.int32, (BLK, BLK), 1)
    for h in range(GROUP):
        q = q_ref[:, h * HD : (h + 1) * HD]
        own = jnp.where(row >= column, nt(q, keys) * SCALE, -jnp.inf)
        first = jnp.where(has_anchor, nt(q, anchor_keys) * SCALE, -jnp.inf)
        top = jnp.max(jnp.maximum(own, first), axis=-1, keepdims=True)
        own, first = jnp.exp(own - top), jnp.exp(first - top)
        total = jnp.sum(own + first, axis=-1, keepdims=True)
        summed = nn(own.astype(BF16), values) + nn(first.astype(BF16), anchor_values)
        out_ref[:, h * HD : (h + 1) * HD] = (summed / total).astype(BF16)


def context(queries, own, half, other):
    return pl.pallas_call(
        context_kernel,
        out_shape=jax.ShapeDtypeStruct((BLK, GROUP * HD), BF16),
        in_specs=[IN_VMEM] * 4,
        cost_estimate=pl.CostEstimate(
            flops=4 * BLK * GROUP * 2 * BLK * HD,
            transcendentals=BLK * GROUP * 2 * BLK,
            bytes_accessed=1 << 20,
        ),
        name="context",
    )(vmem(queries), vmem(own), vmem(half), vmem(other))


def finish_kernel(parts_ref, out_ref):
    for k in range(2):
        summed = jnp.sum(parts_ref[k * 8 : (k + 1) * 8], axis=0)
        out_ref[k * 32 : k * 32 + 16, :] = summed[:, :64].astype(BF16)
        out_ref[k * 32 + 16 : k * 32 + 32, :] = summed[:, 64:].astype(BF16)


def finish(parts):
    return pl.pallas_call(
        finish_kernel,
        out_shape=jax.ShapeDtypeStruct((64, 64), BF16),
        in_specs=[IN_VMEM],
        name="finish",
    )(vmem(parts))


def body(ctx_queries, ctx_keys, ctx_values, query_queries, query_keys, query_values, out_weight):
    own, rows = pack(ctx_keys, ctx_values, query_keys, query_values, out_weight.T, query_queries)
    mate = lax.ppermute(own, "core", [(0, 1), (1, 0)])

    parts = query_parts(rows, own, mate, query_own(rows, own))
    parts = lax.all_to_all(parts.reshape(PEERS, SHARE, FIRST), ("x", "zb", "za"), 0, 0)
    message = merge_parts(parts)
    gathered = lax.all_to_all(message, ("x", "zb", "za"), 0, 0)

    gathered = gathered.reshape(HALF, SECOND)
    sums = project(gathered, own, mate)
    half = anchor_half(gathered)
    sums = lax.all_to_all(sums.reshape(16, 16, 128), ("core", "tp"), 0, 0)
    other = lax.ppermute(half, "core", [(0, 1), (1, 0)])
    ctx_out = context(ctx_queries, own, half, other)
    query_out = finish(sums)
    return (ctx_out, query_out)


def solution(mesh):
    fine = Mesh(mesh.devices.reshape(4, 2, 4, 2, 8), ("za", "zb", "x", "core", "tp"))
    ctx = ("za", "zb", "x", "core")
    return jax.shard_map(
        body,
        mesh=fine,
        in_specs=(
            P(ctx, "tp"),
            P(ctx, "tp"),
            P(ctx, "tp"),
            P(None, "tp"),
            P(ctx, "tp"),
            P(ctx, "tp"),
            P("tp", ctx),
        ),
        out_specs=(P(ctx, "tp"), P("tp", ctx)),
        check_vma=False,
    )
```

```python
import jax
import jax.numpy as jnp
from jax import lax
from jax.experimental import pallas as pl
from jax.experimental.pallas import tpu as pltpu
from jax.sharding import Mesh
from jax.sharding import PartitionSpec as P

HD = 128
GROUP = 4
BLK = 256
QL = 512
SHARE = 8
PEERS = 32
HALF = QL // 2
SCALE = HD**-0.5
F32 = jnp.float32
BF16 = jnp.bfloat16

STATS = GROUP * HD
ANCHOR = STATS + HD
FIRST = ANCHOR + HD
SECOND = GROUP * HD + HD
TAIL = 2 * BLK
WEIGHT = TAIL + 2 * SHARE
PACKED = WEIGHT + GROUP * 64


def nt(a, b):
    return lax.dot_general(a, b, (((1,), (1,)), ((), ())), preferred_element_type=F32)


def nn(a, b):
    return lax.dot_general(a, b, (((1,), (0,)), ((), ())), preferred_element_type=F32)


def vmem(array):
    return pltpu.with_memory_space_constraint(array, pltpu.VMEM)


IN_VMEM = pl.BlockSpec(memory_space=pltpu.VMEM)


def position_of():
    core = lax.axis_index("core")
    return core, ((lax.axis_index("za") * 2 + lax.axis_index("zb")) * 4 + lax.axis_index("x")) * 2 + core


def pack_kernel(keys, values, query_keys, query_values, weight, rows, out_ref, half_ref, tail_ref, sems):
    core, unused = position_of()
    pieces = [
        (keys, out_ref.at[0:BLK]),
        (values, out_ref.at[BLK:TAIL]),
        (rows.at[:, core], half_ref),
        (query_keys, tail_ref.at[0]),
        (query_values, tail_ref.at[1]),
    ]
    for h in range(GROUP):
        start = WEIGHT + h * 64
        pieces.append((weight.at[:, h * HD : (h + 1) * HD], out_ref.at[start : start + 64]))
    copies = [pltpu.make_async_copy(a, b, sems.at[i]) for i, (a, b) in enumerate(pieces)]
    for copy in copies:
        copy.start()
    for copy in copies:
        copy.wait()
    tail = tail_ref[...].astype(F32).reshape(2 * SHARE, HD)
    out_ref[TAIL:WEIGHT, :] = tail.astype(BF16)


def pack(keys, values, query_keys, query_values, weight, rows):
    packed, half = pl.pallas_call(
        pack_kernel,
        out_shape=(pltpu.VMEM((PACKED, HD), BF16), pltpu.VMEM((8, 32, GROUP * HD), BF16)),
        in_specs=[pl.BlockSpec(memory_space=pl.ANY)] * 6,
        out_specs=(IN_VMEM, IN_VMEM),
        scratch_shapes=[pltpu.VMEM((2, SHARE, HD), BF16), pltpu.SemaphoreType.DMA((9,))],
        name="pack",
    )(keys, values, query_keys, query_values, weight, rows.reshape(8, 2, 32, GROUP * HD))
    return packed, half.reshape(HALF, GROUP * HD)


def stacked(rows_ref):
    return jnp.concatenate([rows_ref[:, h * HD : (h + 1) * HD] for h in range(GROUP)], 0)


def spread(column):
    return jnp.broadcast_to(column, (GROUP * HALF, HD))


def own_kernel(rows_ref, own_ref, top_ref, total_ref, summed_ref):
    keys, values = own_ref[0:BLK, :], own_ref[BLK:TAIL, :]
    scores = nt(stacked(rows_ref), keys) * SCALE
    top = jnp.max(scores, axis=-1, keepdims=True)
    weights = jnp.exp(scores - top)
    top_ref[...] = spread(top)
    total_ref[...] = spread(jnp.sum(weights, axis=-1, keepdims=True))
    summed_ref[...] = nn(weights.astype(BF16), values)


def query_own(rows, own):
    return pl.pallas_call(
        own_kernel,
        out_shape=(pltpu.VMEM((GROUP * HALF, HD), F32),) * 3,
        in_specs=[IN_VMEM] * 2,
        out_specs=(IN_VMEM,) * 3,
        name="query_own",
    )(vmem(rows), vmem(own))


def mate_kernel(rows_ref, own_ref, mate_ref, top_ref, total_ref, summed_ref, out_ref):
    core, block = position_of()
    mate = block + 1 - 2 * core
    keys, values = mate_ref[0:BLK, :], mate_ref[BLK:TAIL, :]
    own_tail, mate_tail = own_ref[TAIL:WEIGHT, :].astype(F32), mate_ref[TAIL:WEIGHT, :].astype(F32)
    spare = jnp.zeros((HD - 2 * SHARE, HD), F32)
    tail_keys = jnp.concatenate([own_tail[:SHARE], mate_tail[:SHARE], spare], 0).astype(BF16)
    tail_values = jnp.concatenate([own_tail[SHARE:], mate_tail[SHARE:], spare], 0).astype(BF16)

    index = lax.broadcasted_iota(jnp.int32, (HALF, HD), 0)
    position = (index // 32) * 64 + core * 32 + index % 32
    lane = lax.broadcasted_iota(jnp.int32, (HALF, HD), 1)
    key_position = jnp.where(lane < SHARE, block * SHARE + lane, mate * SHARE + lane - SHARE)
    seen = (lane < 2 * SHARE) & (position >= key_position)
    seen = jnp.concatenate([jnp.where(seen, 0.0, -jnp.inf)] * GROUP, 0)

    q = stacked(rows_ref)
    scores = nt(q, keys) * SCALE
    tail = nt(q, tail_keys) * SCALE + seen
    top1 = jnp.maximum(jnp.maximum(scores[:, :HD], scores[:, HD:]), tail)
    top1 = jnp.max(top1, axis=-1, keepdims=True)
    weights, tail = jnp.exp(scores - top1), jnp.exp(tail - top1)
    total1 = jnp.sum(weights[:, :HD] + weights[:, HD:] + tail, axis=-1, keepdims=True)
    summed1 = nn(weights.astype(BF16), values) + nn(tail.astype(BF16), tail_values)
    top0, top1 = top_ref[...], spread(top1)
    tops = jnp.maximum(top0, top1)
    factor0, factor1 = jnp.exp(top0 - tops), jnp.exp(top1 - tops)
    summed = (summed_ref[...] * factor0 + summed1 * factor1).astype(BF16)
    totals = total_ref[...] * factor0 + spread(total1) * factor1

    stats = jnp.zeros((HALF, HD), F32)
    for h in range(GROUP):
        mine = slice(h * HALF, (h + 1) * HALF)
        out_ref[:, h * HD : (h + 1) * HD] = summed[mine]
        top, total = tops[mine], totals[mine]
        first = top.astype(BF16).astype(F32)
        second = (top - first).astype(BF16).astype(F32)
        high = total.astype(BF16).astype(F32)
        terms = (first, second, top - first - second, high, total - high)
        for i, term in enumerate(terms):
            stats = jnp.where(lane == i * GROUP + h, term, stats)
    out_ref[:, STATS:ANCHOR] = stats.astype(BF16)

    @pl.when(core == 0)
    def _():
        out_ref[:, ANCHOR:FIRST] = own_ref[0:BLK, :]
        pl.delay(2750)

    @pl.when(core != 0)
    def _():
        out_ref[:, ANCHOR:FIRST] = values


def query_parts(rows, own, mate, parts):
    return pl.pallas_call(
        mate_kernel,
        out_shape=pltpu.VMEM((HALF, FIRST), BF16),
        in_specs=[IN_VMEM] * 6,
        out_specs=IN_VMEM,
        name="query_parts",
    )(vmem(rows), vmem(own), vmem(mate), *(vmem(part) for part in parts))


def merge_kernel(parts_ref, out_ref):
    stats = parts_ref[:, :, STATS:ANCHOR].astype(F32)
    flat = stats.reshape(PEERS * SHARE, HD)
    top = flat + (pltpu.roll(flat, HD - GROUP, 1) + pltpu.roll(flat, HD - 2 * GROUP, 1))
    top = top.reshape(PEERS, SHARE, HD)
    factor = jnp.exp(top - jnp.max(top, axis=0, keepdims=True))
    for h in range(GROUP):
        weight = jnp.broadcast_to(factor[:, :, h : h + 1], (PEERS, SHARE, HD))
        totals = jnp.sum(weight * stats, axis=0)
        high, low = 3 * GROUP + h, 4 * GROUP + h
        total = totals[:, high : high + 1] + totals[:, low : low + 1]
        part = parts_ref[:, :, h * HD : (h + 1) * HD].astype(F32)
        attended = (jnp.sum(weight * part, axis=0) / total).astype(BF16)
        out_ref[:, :, h * HD : (h + 1) * HD] = jnp.broadcast_to(attended[None], (PEERS, SHARE, HD))
    anchor = jnp.broadcast_to(parts_ref[0, :, ANCHOR:FIRST][None], (PEERS, SHARE, HD))
    out_ref[:, :, GROUP * HD : (GROUP + 1) * HD] = anchor


def merge_parts(parts):
    return pl.pallas_call(
        merge_kernel,
        out_shape=pltpu.VMEM((PEERS, SHARE, SECOND), BF16),
        in_specs=[IN_VMEM],
        out_specs=IN_VMEM,
        name="merge_parts",
    )(vmem(parts))


def project_kernel(rows_ref, own_ref, mate_ref, out_ref):
    core, unused = position_of()
    rows = rows_ref[:, : GROUP * HD].reshape(8, 2, 16, GROUP * HD)
    upper = rows[:, 0].reshape(128, GROUP * HD)
    lower = rows[:, 1].reshape(128, GROUP * HD)

    def packed(ref):
        pieces = [ref[WEIGHT + h * 64 : WEIGHT + (h + 1) * 64, :] for h in range(GROUP)]
        weight = jnp.concatenate(pieces, 1)
        zero = jnp.zeros_like(weight)
        left = jnp.concatenate([weight, zero], 0)
        right = jnp.concatenate([zero, weight], 0)
        return (nt(upper, left) + nt(lower, right)).reshape(8, 16, 128)

    out_ref[pl.ds(core, 1)] = packed(own_ref)[None]
    out_ref[pl.ds(1 - core, 1)] = packed(mate_ref)[None]


def project(rows, own, mate):
    return pl.pallas_call(
        project_kernel,
        out_shape=pltpu.VMEM((2, 8, 16, 128), F32),
        in_specs=[IN_VMEM] * 3,
        out_specs=IN_VMEM,
        name="project",
    )(vmem(rows), vmem(own), vmem(mate))


def half_kernel(rows_ref, half_ref):
    half_ref[...] = rows_ref[:, GROUP * HD :]


def anchor_half(rows):
    return pl.pallas_call(
        half_kernel,
        out_shape=pltpu.VMEM((BLK, HD), BF16),
        in_specs=[IN_VMEM],
        out_specs=IN_VMEM,
        name="anchor_half",
    )(vmem(rows))


def context_kernel(q_ref, own_ref, half_ref, other_ref, out_ref):
    core, block = position_of()
    has_anchor = block > 0
    half, other = half_ref[...].astype(F32), other_ref[...].astype(F32)
    anchor_keys = jnp.where(core == 0, half, other).astype(BF16)
    anchor_values = jnp.where(core == 0, other, half).astype(BF16)
    keys, values = own_ref[0:BLK, :], own_ref[BLK : 2 * BLK, :]
    row = lax.broadcasted_iota(jnp.int32, (BLK, BLK), 0)
    column = lax.broadcasted_iota(jnp.int32, (BLK, BLK), 1)
    for h in range(GROUP):
        q = q_ref[:, h * HD : (h + 1) * HD]
        own = jnp.where(row >= column, nt(q, keys) * SCALE, -jnp.inf)
        first = jnp.where(has_anchor, nt(q, anchor_keys) * SCALE, -jnp.inf)
        top = jnp.max(jnp.maximum(own, first), axis=-1, keepdims=True)
        own, first = jnp.exp(own - top), jnp.exp(first - top)
        total = jnp.sum(own + first, axis=-1, keepdims=True)
        summed = nn(own.astype(BF16), values) + nn(first.astype(BF16), anchor_values)
        out_ref[:, h * HD : (h + 1) * HD] = (summed / total).astype(BF16)


def context(queries, own, half, other):
    return pl.pallas_call(
        context_kernel,
        out_shape=jax.ShapeDtypeStruct((BLK, GROUP * HD), BF16),
        in_specs=[IN_VMEM] * 4,
        cost_estimate=pl.CostEstimate(
            flops=4 * BLK * GROUP * 2 * BLK * HD,
            transcendentals=BLK * GROUP * 2 * BLK,
            bytes_accessed=1 << 20,
        ),
        name="context",
    )(vmem(queries), vmem(own), vmem(half), vmem(other))


def finish_kernel(parts_ref, out_ref):
    for k in range(2):
        summed = jnp.sum(parts_ref[k * 8 : (k + 1) * 8], axis=0)
        out_ref[k * 32 : k * 32 + 16, :] = summed[:, :64].astype(BF16)
        out_ref[k * 32 + 16 : k * 32 + 32, :] = summed[:, 64:].astype(BF16)


def finish(parts):
    return pl.pallas_call(
        finish_kernel,
        out_shape=jax.ShapeDtypeStruct((64, 64), BF16),
        in_specs=[IN_VMEM],
        name="finish",
    )(vmem(parts))


def body(ctx_queries, ctx_keys, ctx_values, query_queries, query_keys, query_values, out_weight):
    own, rows = pack(ctx_keys, ctx_values, query_keys, query_values, out_weight.T, query_queries)
    mate = lax.ppermute(own, "core", [(0, 1), (1, 0)])

    parts = query_parts(rows, own, mate, query_own(rows, own))
    parts = lax.all_to_all(parts.reshape(PEERS, SHARE, FIRST), ("x", "zb", "za"), 0, 0)
    message = merge_parts(parts)
    gathered = lax.all_to_all(message, ("x", "zb", "za"), 0, 0)

    gathered = gathered.reshape(HALF, SECOND)
    sums = project(gathered, own, mate)
    half = anchor_half(gathered)
    sums = lax.all_to_all(sums.reshape(16, 16, 128), ("core", "tp"), 0, 0)
    other = lax.ppermute(half, "core", [(0, 1), (1, 0)])
    ctx_out = context(ctx_queries, own, half, other)
    query_out = finish(sums)
    return (ctx_out, query_out)


def solution(mesh):
    fine = Mesh(mesh.devices.reshape(4, 2, 4, 2, 8), ("za", "zb", "x", "core", "tp"))
    ctx = ("za", "zb", "x", "core")
    return jax.shard_map(
        body,
        mesh=fine,
        in_specs=(
            P(ctx, "tp"),
            P(ctx, "tp"),
            P(ctx, "tp"),
            P(None, "tp"),
            P(ctx, "tp"),
            P(ctx, "tp"),
            P("tp", ctx),
        ),
        out_specs=(P(ctx, "tp"), P("tp", ctx)),
        check_vma=False,
    )
```
